32 devices in a mesh: dp: 4 (over y, x), ctx: 8 (over z, core).
Axes of the slice: x: 2, y: 2, z: 4, core: 2. Of those that a mesh axis runs over, the one named last changes fastest.
Arguments:
- query_rows: bfloat16 [4096, 4096], P(('dp', 'ctx')), may hold values from -32 to 32
- key_rows: bfloat16 [4096, 512], P(('dp', 'ctx')), may hold values from -8 to 8
- value_rows: bfloat16 [4096, 512], P(('dp', 'ctx')), may hold values from -6 to 6
- out_grad: bfloat16 [4096, 4096], P(('dp', 'ctx')), may hold values from -6 to 6
- destination: int32 [4, 1024], P('dp'), may hold values from 0 to 1023, as said below
- group_first: int32 [4, 8], P('dp', 'ctx'), may hold values from 0 to 7, as said below
Outputs:
- attended: bfloat16 [4096, 4096], P(('dp', 'ctx'))
- grad_query: bfloat16 [4096, 4096], P(('dp', 'ctx'))
- grad_key: bfloat16 [4096, 512], P(('dp', 'ctx'))
- grad_value: bfloat16 [4096, 512], P(('dp', 'ctx'))
- bias_grad: float32 [4608], replicated
The draws below stay inside these ranges and needn't reach their ends.
Inputs may be any that keep to these rules, and one draw needn't show every extreme that they name: For each replica r, destination[r] is a permutation of 0 to 1023. Of the 128 tokens of one index of ctx, at most 32 take slots in any one block, and in every replica some index and block reach 32. group_first[r, b] equals b where a sequence group begins (always at b = 0) and group_first[r, b - 1] otherwise.
All inputs are finite; a program needn't handle non-finite values.
Results may differ from the reference program's by a relative error of at most 0.008.
Values may be sent and summed in bfloat16 or wider, within the bound.
No kernel may reach another device: no remote copies, remote signals or barrier semaphores. Data moves between devices by JAX's collectives and lax.ppermute only.
A program may use at most 64 MiB of HBM per device.

```python
import jax
import jax.numpy as jnp
from jax import lax

ROWS = 128
HD = 128
KVH = 4
GROUP = 8
RUN = 1024
TOKENS = 4096
N_DP = 4
N_CTX = 8


def replica_plan(stream):
    count = N_CTX
    share = ROWS // N_CTX
    parts = jax.random.split(stream, 6)
    order = jax.random.permutation(parts[0], count)
    shifts = jax.random.permutation(parts[1], count)
    spread = jax.random.randint(parts[2], (count // 2,), 0, share + 1).at[0].set(share)
    sizes = jnp.concatenate([share + spread, share - spread])
    sizes = sizes[jax.random.permutation(parts[3], count)]
    ends = jnp.cumsum(sizes)
    places = jnp.arange(ROWS)
    rounds = jnp.sum((places[None, :] >= ends[:, None]).astype(jnp.int32), axis=0)

    def shuffled(stream_one):
        return jax.random.permutation(stream_one, ROWS)
    row_order = jax.vmap(shuffled)(jax.random.split(parts[4], count))
    slot_order = jax.vmap(shuffled)(jax.random.split(parts[5], count))
    ranked = jnp.arange(count)
    sender = order[:, None] + jnp.zeros((1, ROWS), jnp.int32)
    target = order[(ranked[:, None] + shifts[rounds][None, :]) % count]
    values = target * ROWS + slot_order[target, places[None, :]]
    positions = sender * ROWS + row_order[sender, places[None, :]]
    empty = jnp.zeros((count * ROWS,), jnp.int32)
    return empty.at[positions.reshape(-1)].set(values.reshape(-1).astype(jnp.int32))


def all_plans(stream):
    return jax.vmap(replica_plan)(jax.random.split(stream, N_DP))


def drawn(stream):
    queries = jax.random.normal(jax.random.fold_in(stream, 1), (TOKENS, KVH, GROUP, HD), jnp.float32)
    keys_all = jax.random.normal(jax.random.fold_in(stream, 2), (TOKENS, KVH, HD), jnp.float32)
    queries = jnp.clip(queries, -6.0, 6.0)
    keys_all = jnp.clip(keys_all, -6.0, 6.0)
    return (queries, keys_all)


def draw_destination(key, part):
    return all_plans(jax.random.fold_in(key, 7))


def draw_group_first(key, part):
    starts = jax.random.randint(jax.random.fold_in(key, 13), (N_DP, N_CTX), 0, 8) == 0
    offset = jax.random.randint(jax.random.fold_in(key, 14), (N_DP, 1), 0, N_CTX // 2)
    places = jnp.arange(N_CTX, dtype=jnp.int32)
    inside = jnp.logical_and(places[None, :] > offset, places[None, :] < offset + N_CTX // 2)
    starts = jnp.logical_and(starts, jnp.logical_not(inside))
    starts = jnp.logical_or(starts, places[None, :] == 0)
    starts = jnp.logical_or(starts, places[None, :] == offset + N_CTX // 2)
    marked = jnp.where(starts, places[None, :], 0).astype(jnp.int32)
    return lax.cummax(marked, axis=1).astype(jnp.int32)


def draw_query_rows(key, part):
    queries, keys_all = drawn(key)
    return jnp.clip(queries, -32.0, 32.0).reshape(TOKENS, KVH * GROUP * HD).astype(jnp.bfloat16)


def draw_key_rows(key, part):
    queries, keys_all = drawn(key)
    return jnp.clip(keys_all, -8.0, 8.0).reshape(TOKENS, KVH * HD).astype(jnp.bfloat16)


def strengthened(entries, key, source, target, blocks, factor):
    owner, partner = [(jnp.arange(entries.shape[axis_at]) // (entries.shape[axis_at] // blocks)).reshape([-1 if axis == axis_at else 1 for axis in range(entries.ndim)]) for axis_at in (source, target)]
    chosen = jax.random.permutation(key, blocks)[partner]
    strong = (owner == chosen) | (owner == (partner + blocks // 2) % blocks)
    return jnp.where(strong, factor * entries, entries)


def levels(stream_key, shape, shards, least, high):
    factor_of = 1.0
    for dim, blocks in shards:
        steps = jax.random.uniform(jax.random.fold_in(jax.random.fold_in(stream_key, 6), dim), (blocks,), jnp.float32, least / len(shards), high / len(shards))
        factor_of = factor_of * jnp.repeat(jnp.exp(steps), shape[dim] // blocks).reshape((-1,) + (1,) * (len(shape) - 1 - dim))
    return factor_of


def noise(rng, shape, scale, bound, cuts=(), kind=jnp.bfloat16):
    values = jax.random.normal(rng, shape, jnp.float32) * scale
    if len(cuts) > 0:
        values = levels(rng, shape, cuts, -0.22, 0.18) * values
    return jnp.clip(values, min=-bound, max=bound).astype(kind)


def gaussian_with(key, dims, scale, bound, cuts, heavy, kind=jnp.bfloat16):
    result = scale * jax.random.normal(key, dims, jnp.float32)
    if cuts:
        result = result * levels(key, dims, cuts, -0.22, 0.18)
    return jnp.clip(strengthened(result, jax.random.fold_in(key, 3), *heavy), -bound, bound).astype(kind)


def setup_inputs(seed: int = 0) -> dict:
    arg_keys = jax.random.split(jax.random.key(seed), 7)
    return {
        "query_rows": draw_query_rows(jax.random.fold_in(arg_keys[6], 71), 0),
        "key_rows": draw_key_rows(jax.random.fold_in(arg_keys[6], 71), 0),
        "value_rows": noise(arg_keys[2], (TOKENS, KVH * HD), 1.0, 6.0, ((0, 32),)),
        "out_grad": gaussian_with(arg_keys[3], (TOKENS, KVH * GROUP * HD), 1.0, 6.0, ((0, 32),), (0, 1, 32, 2.75)),
        "destination": draw_destination(jax.random.fold_in(arg_keys[6], 71), 0),
        "group_first": draw_group_first(jax.random.fold_in(arg_keys[6], 71), 0),
    }


HIGH = lax.Precision.HIGHEST


def product(form, left, right):
    return jnp.einsum(form, left.astype(jnp.float32), right.astype(jnp.float32), precision=HIGH)


def block_attention(query_own, keys_own, values_own, grads_own, keys_prior, values_prior, linked):
    length = query_own.shape[0]
    scaling = query_own.shape[-1] ** -0.5
    places = jnp.arange(length)
    lower_mask = places[:, None] >= places[None, :]
    upper_mask = jnp.logical_and(places[:, None] >= 0 * places[None, :], linked)
    score_own = jnp.where(lower_mask, product("qhgd,khd->hgqk", query_own, keys_own) * scaling, -jnp.inf)
    score_prior = jnp.where(upper_mask, product("qhgd,khd->hgqk", query_own, keys_prior) * scaling, -jnp.inf)
    ceiling = jnp.maximum(jnp.max(score_own, axis=-1), jnp.max(score_prior, axis=-1))[..., None]
    raw_own = jnp.exp(score_own - ceiling)
    raw_prior = jnp.exp(score_prior - ceiling)
    denom = jnp.sum(raw_own, axis=-1, keepdims=True) + jnp.sum(raw_prior, axis=-1, keepdims=True)
    prob_own = raw_own / denom
    prob_prior = raw_prior / denom
    weight_own = prob_own.astype(jnp.bfloat16)
    weight_prior = prob_prior.astype(jnp.bfloat16)
    attended = (product("hgqk,khd->qhgd", weight_own, values_own)
                + product("hgqk,khd->qhgd", weight_prior, values_prior)).astype(jnp.bfloat16)
    press_own = product("qhgd,khd->hgqk", grads_own, values_own)
    press_prior = product("qhgd,khd->hgqk", grads_own, values_prior)
    centred = (jnp.sum(prob_own * press_own, axis=-1) + jnp.sum(prob_prior * press_prior, axis=-1))[..., None]
    slope_own = (prob_own * (press_own - centred) * scaling).astype(jnp.bfloat16)
    slope_prior = (prob_prior * (press_prior - centred) * scaling).astype(jnp.bfloat16)
    grad_q = (product("hgqk,khd->qhgd", slope_own, keys_own)
              + product("hgqk,khd->qhgd", slope_prior, keys_prior)).astype(jnp.bfloat16)
    key_own = product("hgqk,qhgd->khd", slope_own, query_own).astype(jnp.bfloat16)
    key_prior = product("hgqk,qhgd->khd", slope_prior, query_own).astype(jnp.bfloat16)
    value_own = product("hgqk,qhgd->khd", weight_own, grads_own).astype(jnp.bfloat16)
    value_prior = product("hgqk,qhgd->khd", weight_prior, grads_own).astype(jnp.bfloat16)
    return attended, grad_q, key_own, key_prior, value_own, value_prior


def one_block(pieces):
    return block_attention(pieces[0], pieces[1], pieces[2], pieces[3], pieces[4], pieces[5], pieces[6])


def following(parts):
    return jnp.concatenate([parts[1:], jnp.zeros_like(parts[:1])]).astype(jnp.float32)


def replica(inputs):
    queries, keys_in, values_in, grads_in, plan, firsts = inputs
    inverse = jnp.zeros_like(plan).at[plan].set(jnp.arange(RUN, dtype=jnp.int32))
    query_slots = queries[inverse].reshape(N_CTX, ROWS, KVH, GROUP, HD)
    key_slots = keys_in[inverse].reshape(N_CTX, ROWS, KVH, HD)
    value_slots = values_in[inverse].reshape(N_CTX, ROWS, KVH, HD)
    grad_slots = grads_in[inverse].reshape(N_CTX, ROWS, KVH, GROUP, HD)
    key_before = jnp.concatenate([jnp.zeros_like(key_slots[:1]), key_slots[:-1]])
    value_before = jnp.concatenate([jnp.zeros_like(value_slots[:1]), value_slots[:-1]])
    linked = firsts < jnp.arange(N_CTX, dtype=jnp.int32)
    results = lax.map(one_block, (query_slots, key_slots, value_slots, grad_slots, key_before, value_before, linked))
    attended, grad_q, key_own, key_prior, value_own, value_prior = results
    grad_k = (key_own.astype(jnp.float32) + following(key_prior)).astype(jnp.bfloat16)
    grad_v = (value_own.astype(jnp.float32) + following(value_prior)).astype(jnp.bfloat16)
    wide = KVH * GROUP * HD
    narrow = KVH * HD
    return (attended.reshape(RUN, wide)[plan], grad_q.reshape(RUN, wide)[plan],
            grad_k.reshape(RUN, narrow)[plan], grad_v.reshape(RUN, narrow)[plan])


def reference(query_rows, key_rows, value_rows, out_grad, destination, group_first):
    wide = KVH * GROUP * HD
    narrow = KVH * HD
    results = lax.map(replica, (query_rows.reshape(N_DP, RUN, wide), key_rows.reshape(N_DP, RUN, narrow),
                                value_rows.reshape(N_DP, RUN, narrow), out_grad.reshape(N_DP, RUN, wide),
                                destination, group_first))
    attended = results[0].reshape(TOKENS, wide)
    grad_query = results[1].reshape(TOKENS, wide)
    grad_key = results[2].reshape(TOKENS, narrow)
    grad_value = results[3].reshape(TOKENS, narrow)
    bias_grad = jnp.concatenate([jnp.sum(grad_query.astype(jnp.float32), axis=0),
                                 jnp.sum(grad_value.astype(jnp.float32), axis=0)]) * (TOKENS ** -0.5)
    return attended, grad_query, grad_key, grad_value, bias_grad
```

```python
import functools
import math

import jax
import jax.numpy as jnp
from jax import lax
from jax.experimental import pallas as pl
from jax.experimental.pallas import tpu as pltpu
from jax.sharding import PartitionSpec as P

HD = 128
GROUP = 8
CORES = 2
EXTRA = 8
BIAS_ROWS = 16
NEG = -1e30
LOG2E = math.log2(math.e)


def nn(left, right):
    return lax.dot_general(
        left, right, (((1,), (0,)), ((), ())), preferred_element_type=jnp.float32
    )


def attention_kernel(
    core_ref,
    slot_query,
    slot_key,
    query_own,
    grad_own,
    far_in,
    pairs,
    *refs,
    carried,
):
    if carried:
        refs = refs[2:]
    attended, grad_query, far_out, parts, bias, key_t, value_t, mask, key_sum, value_sum = refs
    count = pairs.shape[0]
    length = query_own.shape[0]
    keys_total = count * length
    scaling = HD ** (-0.5)
    keys = pairs[:, :length, :].reshape(keys_total, HD)
    values = pairs[:, length : 2 * length, :].reshape(keys_total, HD)
    key_t[...] = keys.T
    value_t[...] = values.T
    slot = slot_query[...]
    block = slot // length
    reach = jnp.zeros_like(slot)
    for b in range(count):
        flag = pairs[b, 2 * length : 2 * length + 1, 0:1].astype(jnp.float32)
        linked = (flag > 0.5).astype(jnp.int32)
        reach = reach + jnp.where(block == b, 1, 0) * linked
    first = (block - reach) * length
    key_slot = slot_key[...]
    mask[...] = jnp.where((key_slot <= slot) & (key_slot >= first), 0.0, NEG)
    key_sum[...] = jnp.zeros_like(key_sum)
    value_sum[...] = jnp.zeros_like(value_sum)
    bias[...] = jnp.zeros_like(bias)

    def one_head(g, _):
        at = pl.ds(pl.multiple_of(g * HD, HD), HD)
        query = jnp.concatenate([query_own[:, at], far_in[0, :, at]], axis=0)
        grad = jnp.concatenate([grad_own[:, at], far_in[1, :, at]], axis=0)
        score = nn(query, key_t[...]) * (scaling * LOG2E) + mask[...]
        raw = jnp.exp2(score - jnp.max(score, axis=1, keepdims=True))
        inverse = 1.0 / jnp.sum(raw, axis=1, keepdims=True)
        press = nn(grad, value_t[...])
        prob = raw * inverse
        centred = jnp.sum(prob * press, axis=1, keepdims=True)
        slope = (prob * (press - centred)).astype(jnp.bfloat16)
        weight = prob.astype(jnp.bfloat16)
        out = nn(weight, pairs[:, length : 2 * length, :].reshape(keys_total, HD)).astype(
            jnp.bfloat16
        )
        into = (nn(slope, pairs[:, :length, :].reshape(keys_total, HD)) * scaling).astype(
            jnp.bfloat16
        )
        attended[:, at] = out[:length]
        grad_query[:, at] = into[:length]
        far_out[0, :, at] = out[length:]
        far_out[1, :, at] = into[length:]
        bias[pl.ds(g, 1), :] = jnp.sum(into.astype(jnp.float32), axis=0, keepdims=True)
        key_sum[...] += nn(query.T, slope)
        value_sum[...] += nn(grad.T, weight)
        return 0

    lax.fori_loop(0, GROUP, one_head, 0)
    from_keys = key_sum[...].T * scaling
    from_values = value_sum[...].T
    bias[GROUP : GROUP + 1, :] = jnp.sum(from_values, axis=0, keepdims=True)
    parts[:, :length, :] = from_keys.astype(jnp.bfloat16).reshape(count, length, HD)
    parts[:, length:, :] = from_values.astype(jnp.bfloat16).reshape(count, length, HD)


def attention(core, chunk, chunks, slot_query, slot_key, query, grad, far_in, pairs, carried):
    count = pairs.shape[0]
    length = query.shape[0]
    wide = GROUP * HD
    whole = lambda *shape: pl.BlockSpec(shape, lambda i, c: (0,) * len(shape))
    mine = pl.BlockSpec((length, wide), lambda i, c: (0, chunks * c[0] + chunk))
    out_shape = [
        jax.ShapeDtypeStruct(query.shape, jnp.bfloat16),
        jax.ShapeDtypeStruct(query.shape, jnp.bfloat16),
        jax.ShapeDtypeStruct((2, length, wide), jnp.bfloat16),
        jax.ShapeDtypeStruct((count, 2 * length, HD), jnp.bfloat16),
        jax.ShapeDtypeStruct((BIAS_ROWS, HD), jnp.float32),
    ]
    rows = CORES * length
    cols = count * length
    in_specs = [
        whole(rows, 1),
        whole(1, cols),
        mine,
        mine,
        whole(2, length, wide),
        whole(*pairs.shape),
    ]
    operands = [slot_query, slot_key, query, grad, far_in, pairs]
    aliases = {}
    if carried is not None:
        in_specs += [pl.BlockSpec(memory_space=pl.ANY)] * 2
        aliases = {7: 0, 8: 1}
        operands += list(carried)
    grid_spec = pltpu.PrefetchScalarGridSpec(
        num_scalar_prefetch=1,
        grid=(1,),
        in_specs=in_specs,
        out_specs=[
            mine,
            mine,
            whole(2, length, wide),
            whole(count, 2 * length, HD),
            whole(BIAS_ROWS, HD),
        ],
        scratch_shapes=[
            pltpu.VMEM((HD, cols), jnp.bfloat16),
            pltpu.VMEM((HD, cols), jnp.bfloat16),
            pltpu.VMEM((rows, cols), jnp.float32),
            pltpu.VMEM((HD, cols), jnp.float32),
            pltpu.VMEM((HD, cols), jnp.float32),
        ],
    )
    work = rows * GROUP * cols
    return pl.pallas_call(
        functools.partial(attention_kernel, carried=carried is not None),
        grid_spec=grid_spec,
        out_shape=out_shape,
        input_output_aliases=aliases,
        compiler_params=pltpu.CompilerParams(vmem_limit_bytes=60 * 1024 * 1024),
        cost_estimate=pl.CostEstimate(
            flops=12 * work * HD, transcendentals=work, bytes_accessed=8 * length * wide * 2
        ),
        name="attention",
    )(core, *operands)


def place_kernel(core_ref, first, second, attended_in, grad_in, attended, grad_query):
    for at, source in enumerate((first, second)):

        @pl.when(pl.program_id(0) == at)
        def _():
            attended[...] = source[0]
            grad_query[...] = source[1]


def place(core, swapped, attended, grad_query):
    chunks = len(swapped)
    _, length, wide = swapped[0].shape
    theirs = pl.BlockSpec((length, wide), lambda i, c: (0, chunks * (1 - c[0]) + i))
    grid_spec = pltpu.PrefetchScalarGridSpec(
        num_scalar_prefetch=1,
        grid=(chunks,),
        in_specs=[pl.BlockSpec((2, length, wide), lambda i, c: (0, 0, 0))] * chunks
        + [pl.BlockSpec(memory_space=pl.ANY)] * 2,
        out_specs=[theirs, theirs],
    )
    return pl.pallas_call(
        place_kernel,
        grid_spec=grid_spec,
        out_shape=[jax.ShapeDtypeStruct(attended.shape, attended.dtype)] * 2,
        input_output_aliases={3: 0, 4: 1},
        name="place",
    )(core, *swapped, attended, grad_query)


def finish_kernel(*refs):
    *pieces, grad_key, grad_value = refs
    chunks = len(pieces)
    length = grad_key.shape[0]
    for hh, piece in enumerate(pieces):
        for c in range(CORES):
            total = piece[c].astype(jnp.float32)
            for z in range(1, piece.shape[0] // CORES):
                total = total + piece[CORES * z + c].astype(jnp.float32)
            total = total.astype(jnp.bfloat16)
            at = slice((c * chunks + hh) * HD, (c * chunks + hh + 1) * HD)
            grad_key[:, at] = total[:length]
            grad_value[:, at] = total[length:]


def finish(pieces, shape):
    return pl.pallas_call(
        finish_kernel,
        out_shape=[jax.ShapeDtypeStruct(shape, jnp.bfloat16)] * 2,
        name="finish",
    )(*pieces)


def doubled(part, axis):
    size = lax.axis_size(axis)
    step = 1
    while step < size:
        part = part + lax.ppermute(part, axis, [(i, i ^ step) for i in range(size)])
        step *= 2
    return part


def local(query_rows, key_rows, value_rows, out_grad, destination, group_first):
    length = query_rows.shape[0]
    devices = lax.axis_size("ctx")
    replicas = lax.axis_size("dp")
    index = lax.axis_index("ctx")
    core = index % CORES
    kv_heads = key_rows.shape[1] // HD
    chunks = kv_heads // CORES
    wide = GROUP * HD
    plan = destination[0]
    flag = jnp.where(group_first[0, 0] < index, 1.0, 0.0).astype(jnp.bfloat16)
    flags = jnp.broadcast_to(flag, (EXTRA, HD))
    across = [(i, i ^ 1) for i in range(devices)]
    core_arg = core.astype(jnp.int32).reshape(1)

    gathered = []
    swapped_in = []
    for hh in range(chunks):
        blocks = []
        for c in range(CORES):
            head = c * chunks + hh
            at = slice(head * HD, (head + 1) * HD)
            blocks.append(jnp.concatenate([key_rows[:, at], value_rows[:, at], flags], axis=0))
        outgoing = jnp.stack(blocks * (devices // CORES))
        gathered.append(lax.all_to_all(outgoing, "ctx", split_axis=0, concat_axis=0, tiled=True))
        start = ((1 - core) * chunks + hh) * wide
        halves = jnp.stack(
            [
                lax.dynamic_slice_in_dim(query_rows, start, wide, axis=1),
                lax.dynamic_slice_in_dim(out_grad, start, wide, axis=1),
            ]
        )
        swapped_in.append(lax.ppermute(halves, "ctx", across))
    slot_own = lax.dynamic_slice_in_dim(plan, index * length, length)
    slot_far = lax.dynamic_slice_in_dim(plan, (index ^ 1) * length, length)
    slot_query = jnp.concatenate([slot_own, slot_far]).reshape(CORES * length, 1)
    slot_key = plan.reshape(1, devices * length)

    carried = None
    returned = []
    swapped_out = []
    sums = []
    for hh in range(chunks):
        attended, grad_query, far, parts, bias = attention(
            core_arg,
            hh,
            chunks,
            slot_query,
            slot_key,
            query_rows,
            out_grad,
            swapped_in[hh],
            gathered[hh],
            carried,
        )
        carried = (attended, grad_query)
        returned.append(lax.all_to_all(parts, "ctx", split_axis=0, concat_axis=0, tiled=True))
        swapped_out.append(lax.ppermute(far, "ctx", across))
        sums.append(bias)
    attended, grad_query = place(core_arg, swapped_out, *carried)
    partial = doubled(jnp.stack(sums), "dp")
    spread = lax.all_to_all(
        jnp.broadcast_to(partial[None], (devices,) + partial.shape),
        "ctx",
        split_axis=0,
        concat_axis=0,
        tiled=True,
    )
    grad_key, grad_value = finish(returned, key_rows.shape)
    total = jnp.sum(spread.reshape((devices // CORES, CORES) + partial.shape), axis=0)
    total = total.reshape(kv_heads, BIAS_ROWS, HD)
    bias_grad = jnp.concatenate(
        [total[:, :GROUP].reshape(-1), total[:, GROUP].reshape(-1)]
    ) * (1.0 / math.sqrt(length * devices * replicas))
    return (attended, grad_query, grad_key, grad_value, bias_grad)


def solution(mesh):
    rows = P(("dp", "ctx"), None)
    return jax.shard_map(
        local,
        mesh=mesh,
        in_specs=(rows, rows, rows, rows, P("dp", None), P("dp", "ctx")),
        out_specs=(rows, rows, rows, rows, P()),
        check_vma=False,
    )
```

```python
import functools
import math

import jax
import jax.numpy as jnp
from jax import lax
from jax.experimental import pallas as pl
from jax.experimental.pallas import tpu as pltpu
from jax.sharding import PartitionSpec as P


HD = 128
GROUP = 8
CORES = 2
EXTRA = 8
BIAS_ROWS = 16
NEG = -1e30
SPLIT = (True, False)
LOG2E = math.log2(math.e)


def nn(left, right):
    return lax.dot_general(
        left, right, (((1,), (0,)), ((), ())), preferred_element_type=jnp.float32
    )


def column(row):
    length = row.shape[1]
    down = lax.broadcasted_iota(jnp.int32, (length, length), 0)
    along = lax.broadcasted_iota(jnp.int32, (length, length), 1)
    spread = jnp.where(down == along, row.astype(jnp.float32), 0.0)
    return jnp.sum(spread, axis=1, keepdims=True).astype(jnp.int32)


def attention_kernel(index_ref, plan, query_own, grad_own, far_in, *refs, carried, split):
    chips = plan.shape[0] // CORES
    pairs = refs[:chips]
    refs = refs[chips + (4 if carried else 0) :]
    attended, grad_query, bias, far_out = refs[:4]
    parts = refs[4 : 4 + (chips if split else 1)]
    key_t, value_t, mask, key_sum, value_sum, *work = refs[4 + len(parts) :]
    score_refs, press_refs, weight_refs, slope_refs = (work[k : k + 2] for k in (0, 2, 4, 6))
    count = plan.shape[0]
    length = query_own.shape[0]
    scaling = HD ** (-0.5)

    def gathered(start):
        found = [p[j, start : start + length, :] for p in pairs for j in range(CORES)]
        return jnp.concatenate(found, axis=0)

    key_t[...] = gathered(0).T
    value_t[...] = gathered(length).T
    index = index_ref[0]
    slot = jnp.concatenate(
        [column(plan[pl.ds(index, 1), :]), column(plan[pl.ds(index ^ 1, 1), :])], axis=0
    )
    block = slot // length
    reach = jnp.zeros_like(slot)
    for r in range(count):
        flag = pairs[r // CORES][r % CORES, 2 * length : 2 * length + 1, 0:1]
        linked = (flag.astype(jnp.float32) > 0.5).astype(jnp.int32)
        reach = reach + jnp.where(block == (index ^ r), 1, 0) * linked
    first = (block - reach) * length
    for r in range(count):
        key_slot = plan[pl.ds(index ^ r, 1), :]
        mask[:, r * length : (r + 1) * length] = jnp.where(
            (key_slot <= slot) & (key_slot >= first), 0.0, NEG
        )
    key_sum[...] = jnp.zeros_like(key_sum)
    value_sum[...] = jnp.zeros_like(value_sum)
    bias[...] = jnp.zeros_like(bias)

    def pick(own, far, g):
        at = pl.ds(pl.multiple_of(g * HD, HD), HD)
        return jnp.concatenate([own[:, at], far_in[far, :, at]], axis=0)

    def before(g, s):
        score_refs[s][...] = nn(pick(query_own, 0, g), key_t[...])
        press_refs[s][...] = nn(pick(grad_own, 1, g), value_t[...])

    def during(s):
        for r in range(0, 2 * length, 32):
            rows = slice(r, r + 32)
            score = score_refs[s][rows, :] * (scaling * LOG2E) + mask[rows, :]
            raw = jnp.exp2(score - jnp.max(score, axis=1, keepdims=True))
            prob = raw * (1.0 / jnp.sum(raw, axis=1, keepdims=True))
            press = press_refs[s][rows, :]
            centred = jnp.sum(prob * press, axis=1, keepdims=True)
            weight_refs[s][rows, :] = prob.astype(jnp.bfloat16)
            slope_refs[s][rows, :] = (prob * (press - centred)).astype(jnp.bfloat16)

    def after(g, s):
        at = pl.ds(pl.multiple_of(g * HD, HD), HD)
        weight = weight_refs[s][...]
        slope = slope_refs[s][...]
        out = nn(weight, gathered(length)).astype(jnp.bfloat16)
        into = (nn(slope, gathered(0)) * scaling).astype(jnp.bfloat16)
        attended[:, at] = out[:length]
        grad_query[:, at] = into[:length]
        far_out[0, :, at] = out[length:]
        far_out[1, :, at] = into[length:]
        bias[pl.ds(g, 1), :] = jnp.sum(into.astype(jnp.float32), axis=0, keepdims=True)
        key_sum[...] += nn(pick(query_own, 0, g).T, slope)
        value_sum[...] += nn(pick(grad_own, 1, g).T, weight)


    def two_heads(j, _):
        g = 2 * j
        before(g, 0)
        before(g + 1, 1)
        during(0)
        during(1)
        after(g, 0)
        after(g + 1, 1)
        return 0

    lax.fori_loop(0, GROUP // 2, two_heads, 0)

    from_keys = key_sum[...].T * scaling
    from_values = value_sum[...].T
    bias[GROUP : GROUP + 1, :] = jnp.sum(from_values, axis=0, keepdims=True)
    for r in range(count):
        rows = slice(r * length, (r + 1) * length)
        both = jnp.concatenate([from_keys[rows], from_values[rows]], axis=0)
        both = both.astype(jnp.bfloat16)
        if split:
            parts[r // CORES][r % CORES] = both
        else:
            parts[0][pl.ds(index ^ r, 1)] = both[None]


def attention(index, chunk, chunks, plan, query, grad, far_in, pairs, carried, split):
    count = plan.shape[0]
    chips = count // CORES
    length = query.shape[0]
    wide = GROUP * HD
    whole = lambda *shape: pl.BlockSpec(shape, lambda i, c: (0,) * len(shape))
    mine = pl.BlockSpec((length, wide), lambda i, c: (0, chunks * (c[0] % CORES) + chunk))
    out_shape = [
        jax.ShapeDtypeStruct(query.shape, jnp.bfloat16),
        jax.ShapeDtypeStruct(query.shape, jnp.bfloat16),
        jax.ShapeDtypeStruct((chunks * BIAS_ROWS, HD), jnp.float32),
        jax.ShapeDtypeStruct((2, length, chunks * wide), jnp.bfloat16),
    ]
    part = (CORES, 2 * length, HD) if split else (count, 2 * length, HD)
    parts = chips if split else 1
    out_shape += [jax.ShapeDtypeStruct(part, jnp.bfloat16)] * parts
    rows = CORES * length
    cols = count * length
    far = pl.BlockSpec((2, length, wide), lambda i, c: (0, 0, chunk))
    in_specs = [whole(*plan.shape), mine, mine, far]
    in_specs += [whole(*pairs[0].shape)] * chips
    operands = [plan, query, grad, far_in, *pairs]
    aliases = {}
    if carried is not None:
        in_specs += [pl.BlockSpec(memory_space=pl.ANY)] * 4
        aliases = {5 + chips + k: k for k in range(4)}
        operands += list(carried)
    grid_spec = pltpu.PrefetchScalarGridSpec(
        num_scalar_prefetch=1,
        grid=(1,),
        in_specs=in_specs,
        out_specs=[
            mine,
            mine,
            pl.BlockSpec((BIAS_ROWS, HD), lambda i, c: (chunk, 0)),
            far,
        ]
        + [whole(*part)] * parts,
        scratch_shapes=[
            pltpu.VMEM((HD, cols), jnp.bfloat16),
            pltpu.VMEM((HD, cols), jnp.bfloat16),
            pltpu.VMEM((rows, cols), jnp.float32),
            pltpu.VMEM((HD, cols), jnp.float32),
            pltpu.VMEM((HD, cols), jnp.float32),
        ]
        + [pltpu.VMEM((rows, cols), jnp.float32)] * 4
        + [pltpu.VMEM((rows, cols), jnp.bfloat16)] * 4
        + [
        ],
    )
    work = rows * GROUP * cols
    return pl.pallas_call(
        functools.partial(attention_kernel, carried=carried is not None, split=split),
        grid_spec=grid_spec,
        out_shape=out_shape,
        input_output_aliases=aliases,
        compiler_params=pltpu.CompilerParams(
            vmem_limit_bytes=min(60, 8 + 10 * cols // 1024) * 1024 * 1024
        ),
        cost_estimate=pl.CostEstimate(
            flops=12 * work * HD, transcendentals=work, bytes_accessed=8 * length * wide * 2
        ),
        name="attention",
    )(index, *operands)


def payload_kernel(index_ref, first_ref, keys, values, near, away):
    chunks, _, _ = near.shape
    length = keys.shape[0]
    index = index_ref[0]
    linked = (first_ref[0, 0] < index).astype(jnp.float32)
    flags = jnp.full((EXTRA, HD), linked, jnp.float32).astype(jnp.bfloat16)
    even = index % CORES == 0
    for hh in range(chunks):
        heads = [slice((c * chunks + hh) * HD, (c * chunks + hh + 1) * HD) for c in range(CORES)]
        for at, source in ((0, keys), (length, values)):
            first, second = source[:, heads[0]], source[:, heads[1]]
            near[hh, at : at + length, :] = jnp.where(even, first, second)
            away[hh, at : at + length, :] = jnp.where(even, second, first)
        near[hh, 2 * length :, :] = flags
        away[hh, 2 * length :, :] = flags


def payload(index, group_first, keys, values, chunks):
    length = keys.shape[0]
    smem = pl.BlockSpec(memory_space=pltpu.SMEM)
    vmem = pl.BlockSpec(memory_space=pltpu.VMEM)
    shape = jax.ShapeDtypeStruct((chunks, 2 * length + EXTRA, HD), jnp.bfloat16)
    return pl.pallas_call(
        payload_kernel,
        in_specs=[smem, smem, vmem, vmem],
        out_shape=[shape] * 2,
        name="payload",
    )(index, group_first, keys, values)


def join_kernel(near, away, *outs):
    for hh, out in enumerate(outs):
        out[0] = near[hh]
        out[1] = away[hh]


def join(near, away):
    chunks, rows, _ = near.shape
    shape = jax.ShapeDtypeStruct((CORES, rows, HD), jnp.bfloat16)
    return pl.pallas_call(join_kernel, out_shape=[shape] * chunks, name="join")(near, away)


def place_kernel(index_ref, far, attended_in, grad_in, attended, grad_query):
    attended[...] = far[0]
    grad_query[...] = far[1]


def place(index, far, attended, grad_query):
    _, length, half = far.shape
    theirs = pl.BlockSpec((length, half), lambda i, c: (0, 1 - c[0] % CORES))
    grid_spec = pltpu.PrefetchScalarGridSpec(
        num_scalar_prefetch=1,
        grid=(1,),
        in_specs=[pl.BlockSpec((2, length, half), lambda i, c: (0, 0, 0))]
        + [pl.BlockSpec(memory_space=pl.ANY)] * 2,
        out_specs=[theirs, theirs],
    )
    return pl.pallas_call(
        place_kernel,
        grid_spec=grid_spec,
        out_shape=[jax.ShapeDtypeStruct(attended.shape, attended.dtype)] * 2,
        input_output_aliases={2: 0, 3: 1},
        compiler_params=pltpu.CompilerParams(vmem_limit_bytes=8 * 1024 * 1024),
        name="place",
    )(index, far, attended, grad_query)


def halves_kernel(index_ref, query, grad, out):
    out[0] = query[...]
    out[1] = grad[...]


def halves(index, query, grad):
    length, width = query.shape
    theirs = pl.BlockSpec((length, width // CORES), lambda i, c: (0, 1 - c[0] % CORES))
    grid_spec = pltpu.PrefetchScalarGridSpec(
        num_scalar_prefetch=1,
        grid=(1,),
        in_specs=[theirs, theirs],
        out_specs=pl.BlockSpec((2, length, width // CORES), lambda i, c: (0, 0, 0)),
    )
    return pl.pallas_call(
        halves_kernel,
        grid_spec=grid_spec,
        out_shape=jax.ShapeDtypeStruct((2, length, width // CORES), query.dtype),
        name="halves",
    )(index, query, grad)


def added(pieces):
    total = pieces[0].astype(jnp.float32)
    for piece in pieces[1:]:
        total = total + piece.astype(jnp.float32)
    return total.astype(jnp.bfloat16)


def finish_kernel(index_ref, piece, *refs):
    grad_key, grad_value = refs[-2:]
    length = grad_key.shape[0]
    total = added([piece[z, 0] for z in range(piece.shape[0])])
    grad_key[...] = total[:length]
    grad_value[...] = total[length:]


def settle_kernel(index_ref, *refs, count):
    grad_key, grad_value, away = refs[-3:]
    length = grad_key.shape[0]
    total = added([piece[0] for piece in refs[:count]])
    grad_key[...] = total[:length]
    grad_value[...] = total[length:]
    away[...] = added([piece[1] for piece in refs[:count]])


def into_grads(kernel, index, grid, specs, operands, heads, shape, extra, carried):
    specs = list(specs)
    aliases = {}
    if carried is not None:
        specs += [pl.BlockSpec(memory_space=pl.ANY)] * 2
        aliases = {1 + len(operands): 0, 2 + len(operands): 1}
        operands = [*operands, *carried]
    block = pl.BlockSpec((shape[0], HD), heads)
    out_specs = [block, block]
    out_shape = [jax.ShapeDtypeStruct(shape, jnp.bfloat16)] * 2
    if extra is not None:
        out_specs.append(pl.BlockSpec(extra, lambda i, c: (0,) * len(extra)))
        out_shape.append(jax.ShapeDtypeStruct(extra, jnp.bfloat16))
    grid_spec = pltpu.PrefetchScalarGridSpec(
        num_scalar_prefetch=1, grid=(grid,), in_specs=specs, out_specs=out_specs
    )
    return pl.pallas_call(
        kernel,
        grid_spec=grid_spec,
        out_shape=out_shape,
        input_output_aliases=aliases,
        compiler_params=pltpu.CompilerParams(vmem_limit_bytes=8 * 1024 * 1024),
    )(index, *operands)


def finish(index, chunk, chunks, piece, shape, carried):
    count, rows, _ = piece.shape
    piece = piece.reshape(count // CORES, CORES, rows, HD)
    spec = pl.BlockSpec((count // CORES, 1, rows, HD), lambda i, c: (0, i, 0, 0))
    heads = lambda i, c: (0, i * chunks + chunk)
    return into_grads(finish_kernel, index, CORES, [spec], [piece], heads, shape, None, carried)


def settle(index, chunk, chunks, pieces, shape, carried):
    spec = pl.BlockSpec(pieces[0].shape, lambda i, c: (0, 0, 0))
    heads = lambda i, c: (0, (c[0] % CORES) * chunks + chunk)
    kernel = functools.partial(settle_kernel, count=len(pieces))
    extra = pieces[0].shape[1:]
    return into_grads(kernel, index, 1, [spec] * len(pieces), pieces, heads, shape, extra, carried)


def receive(index, chunk, chunks, piece, shape, carried):
    piece = piece[None, None]
    spec = pl.BlockSpec(piece.shape, lambda i, c: (0, 0, 0, 0))
    heads = lambda i, c: (0, (1 - c[0] % CORES) * chunks + chunk)
    return into_grads(finish_kernel, index, 1, [spec], [piece], heads, shape, None, carried)


def bias_kernel(index_ref, sums, bias_grad, *, chunks, factor):
    core = index_ref[0] % CORES
    for c in range(CORES):
        ours = core == c
        for hh in range(chunks):
            head = c * chunks + hh
            rows = slice(hh * BIAS_ROWS, hh * BIAS_ROWS + GROUP)
            bias_grad[head * GROUP : (head + 1) * GROUP, :] = (
                jnp.where(ours, sums[0, rows, :], sums[1, rows, :]) * factor
            )
            row = slice(hh * BIAS_ROWS + GROUP, hh * BIAS_ROWS + GROUP + 1)
            at = CORES * chunks * GROUP + head
            bias_grad[at : at + 1, :] = (
                jnp.where(ours, sums[0, row, :], sums[1, row, :]) * factor
            )


def bias_total(index, sums, chunks, factor):
    return pl.pallas_call(
        functools.partial(bias_kernel, chunks=chunks, factor=factor),
        in_specs=[
            pl.BlockSpec(memory_space=pltpu.SMEM),
            pl.BlockSpec(memory_space=pltpu.VMEM),
        ],
        out_shape=jax.ShapeDtypeStruct((CORES * chunks * (GROUP + 1), HD), jnp.float32),
        compiler_params=pltpu.CompilerParams(vmem_limit_bytes=4 * 1024 * 1024),
        name="bias",
    )(index, sums)


def summed(part, axis, steps):
    size = lax.axis_size(axis)
    if len(steps) > 2:
        for step in steps:
            part = part + lax.ppermute(part, axis, [(i, i ^ step) for i in range(size)])
        return part
    total = part
    for pick in range(1, 2 ** len(steps)):
        mixed = sum(step for k, step in enumerate(steps) if pick >> k & 1)
        total = total + lax.ppermute(part, axis, [(i, i ^ mixed) for i in range(size)])
    return total


def powers(start, stop):
    found = []
    while start < stop:
        found.append(start)
        start *= 2
    return found


def body(query_rows, key_rows, value_rows, out_grad, destination, group_first):
    length = query_rows.shape[0]
    devices = lax.axis_size("ctx")
    replicas = lax.axis_size("dp")
    index = lax.axis_index("ctx").astype(jnp.int32)
    kv_heads = key_rows.shape[1] // HD
    chunks = kv_heads // CORES
    plan = destination.reshape(devices, length)
    across = [(i, i ^ 1) for i in range(devices)]
    index_arg = index.reshape(1)

    chips = devices // CORES
    order = range(chips - 1, 0, -1)

    def over(k):
        return [(i, i ^ (CORES * k)) for i in range(devices)]

    near, away = payload(index_arg, group_first, key_rows, value_rows, chunks)
    away = lax.ppermute(away, "ctx", across)
    joined = join(near, away)
    gathered = []
    for hh in range(chunks):
        pairs = [joined[hh]] * chips
        for k in order:
            pairs[k] = lax.ppermute(joined[hh], "ctx", over(k))
        gathered.append(pairs)
    far_in = halves(index_arg, query_rows, out_grad)
    far_in = lax.ppermute(far_in, "ctx", across)

    carried = None
    returned = []
    for hh in range(chunks):
        split = SPLIT[hh % len(SPLIT)]
        outs = attention(
            index_arg,
            hh,
            chunks,
            plan,
            query_rows,
            out_grad,
            far_in,
            gathered[hh],
            carried,
            split,
        )
        carried, parts = outs[:4], outs[4:]
        if split:
            pieces = list(parts)
            for k in order:
                pieces[k] = lax.ppermute(parts[k], "ctx", over(k))
            returned.append(pieces)
        else:
            returned.append(
                lax.all_to_all(parts[0], "ctx", split_axis=0, concat_axis=0, tiled=True)
            )
    attended, grad_query, bias, far_out = carried
    far_out = lax.ppermute(far_out, "ctx", across)
    attended, grad_query = place(index_arg, far_out, attended, grad_query)
    both = jnp.stack([bias, lax.ppermute(bias, "ctx", across)])
    both = summed(both, "dp", powers(1, replicas))
    both = summed(both, "ctx", powers(CORES, devices))
    factor = 1.0 / math.sqrt(length * devices * replicas)
    bias_grad = bias_total(index_arg, both, chunks, factor)
    grads = None
    shape = key_rows.shape
    for hh in range(chunks):
        if SPLIT[hh % len(SPLIT)]:
            *grads, away = settle(index_arg, hh, chunks, returned[hh], shape, grads)
            away = lax.ppermute(away, "ctx", across)
            grads = receive(index_arg, hh, chunks, away, shape, grads)
        else:
            grads = finish(index_arg, hh, chunks, returned[hh], shape, grads)
    return (attended, grad_query, *grads, bias_grad.reshape(-1))


def solution(mesh):
    rows = P(("dp", "ctx"), None)
    return jax.shard_map(
        body,
        mesh=mesh,
        in_specs=(rows, rows, rows, rows, P("dp", None), P("dp", "ctx")),
        out_specs=(rows, rows, rows, rows, P()),
        check_vma=False,
    )
```

```python
import functools
import math

import jax
import jax.numpy as jnp
from jax import lax
from jax.experimental import pallas as pl
from jax.experimental.pallas import tpu as pltpu
from jax.sharding import PartitionSpec as P


HD = 128
GROUP = 8
CORES = 2
EXTRA = 8
BIAS_ROWS = 16
NEG = -1e30
VMEM_MIB = 40
ROW_TILE = 32
JOIN = (False, True)
SPLIT = (True, False)
LOG2E = math.log2(math.e)


def nn(left, right):
    return lax.dot_general(
        left, right, (((1,), (0,)), ((), ())), preferred_element_type=jnp.float32
    )


def column(row):
    length = row.shape[1]
    down = lax.broadcasted_iota(jnp.int32, (length, length), 0)
    along = lax.broadcasted_iota(jnp.int32, (length, length), 1)
    spread = jnp.where(down == along, row.astype(jnp.float32), 0.0)
    return jnp.sum(spread, axis=1, keepdims=True).astype(jnp.int32)


def lying(upright):
    length = upright.shape[0]
    down = lax.broadcasted_iota(jnp.int32, (length, length), 0)
    along = lax.broadcasted_iota(jnp.int32, (length, length), 1)
    return jnp.sum(jnp.where(down == along, upright, 0.0), axis=0, keepdims=True)


def attention_kernel(index_ref, plan, near_in, far_in, *refs, carried, split, joined):
    count, length = plan.shape
    chips = count // CORES
    blocks = chips if joined else count
    pairs = refs[:blocks]
    if joined:
        pairs = [p.at[j] for p in pairs for j in range(CORES)]
    refs = refs[blocks + (4 if carried else 0) :]
    attended, grad_query, bias, far_out = refs[:4]
    parts = refs[4 : 4 + (chips if split else 1)]
    key_t, value_t, mask, key_sum, value_sum, *work = refs[4 + len(parts) :]
    score_ref, press_ref, weight_ref, slope_ref = work
    pack = score_ref.shape[0] // (CORES * length)
    scaling = HD ** (-0.5)

    def gathered(start):
        return jnp.concatenate([p[start : start + length, :] for p in pairs], axis=0)

    key_t[...] = gathered(0).T
    value_t[...] = gathered(length).T
    index = index_ref[0]
    slot = jnp.concatenate(
        [column(plan[pl.ds(index, 1), :]), column(plan[pl.ds(index ^ 1, 1), :])], axis=0
    )
    block = slot // length
    reach = jnp.zeros_like(slot)
    for r in range(count):
        flag = pairs[r][2 * length : 2 * length + 1, 0:1]
        linked = (flag.astype(jnp.float32) > 0.5).astype(jnp.int32)
        reach = reach + jnp.where(block == (index ^ r), 1, 0) * linked
    first = (block - reach) * length
    for r in range(count):
        key_slot = plan[pl.ds(index ^ r, 1), :]
        mask[:, r * length : (r + 1) * length] = jnp.where(
            (key_slot <= slot) & (key_slot >= first), 0.0, NEG
        )
    key_sum[...] = jnp.zeros_like(key_sum)
    value_sum[...] = jnp.zeros_like(value_sum)
    bias[...] = jnp.zeros_like(bias)

    def pick(which, g):
        found = []
        for k in range(pack):
            at = pl.ds(pl.multiple_of((g + k) * HD, HD), HD)
            found += [near_in[which, :, at], far_in[which, :, at]]
        return jnp.concatenate(found, axis=0)

    def heads(j, _):
        g = j * pack
        query = pick(0, g)
        grad = pick(1, g)
        score_ref[...] = nn(query, key_t[...])
        press_ref[...] = nn(grad, value_t[...])
        span = CORES * length
        for r in range(0, pack * span, ROW_TILE):
            rows = slice(r, r + ROW_TILE)
            at = slice(r % span, r % span + ROW_TILE)
            score = score_ref[rows, :] * (scaling * LOG2E) + mask[at, :]
            raw = jnp.exp2(score - jnp.max(score, axis=1, keepdims=True))
            prob = raw * (1.0 / jnp.sum(raw, axis=1, keepdims=True))
            press = press_ref[rows, :]
            centred = jnp.sum(prob * press, axis=1, keepdims=True)
            weight_ref[rows, :] = prob.astype(jnp.bfloat16)
            slope_ref[rows, :] = (prob * (press - centred)).astype(jnp.bfloat16)
        weight = weight_ref[...]
        slope = slope_ref[...]
        out = nn(weight, gathered(length)).astype(jnp.bfloat16)
        into = (nn(slope, gathered(0)) * scaling).astype(jnp.bfloat16)
        for k in range(pack):
            at = pl.ds(pl.multiple_of((g + k) * HD, HD), HD)
            near = slice(k * span, k * span + length)
            away = slice(k * span + length, (k + 1) * span)
            attended[:, at] = out[near]
            grad_query[:, at] = into[near]
            far_out[0, :, at] = out[away]
            far_out[1, :, at] = into[away]
            total = jnp.sum(into[k * span : (k + 1) * span].astype(jnp.float32), axis=0)
            bias[pl.ds(g + k, 1), :] = total[None]
        key_sum[...] += nn(query.T, slope)
        value_sum[...] += nn(grad.T, weight)
        return 0

    lax.fori_loop(0, GROUP // pack, heads, 0)
    from_values = value_sum[...]
    bias[GROUP : GROUP + 1, :] = lying(jnp.sum(from_values, axis=1, keepdims=True))
    from_keys = (key_sum[...] * scaling).astype(jnp.bfloat16)
    from_values = from_values.astype(jnp.bfloat16)
    for r in range(count):
        cols = slice(r * length, (r + 1) * length)
        if split:
            parts[r // CORES][r % CORES, :HD, :] = from_keys[:, cols]
            parts[r // CORES][r % CORES, HD:, :] = from_values[:, cols]
        else:
            parts[0][index ^ r, :HD, :] = from_keys[:, cols]
            parts[0][index ^ r, HD:, :] = from_values[:, cols]


def attention(index, chunk, chunks, plan, near_in, far_in, pairs, carried, split):
    count = plan.shape[0]
    chips = count // CORES
    _, length, half = near_in.shape
    wide = GROUP * HD
    whole = lambda *shape: pl.BlockSpec(shape, lambda i, c: (0,) * len(shape))
    mine = pl.BlockSpec((length, wide), lambda i, c: (0, chunks * (c[0] % CORES) + chunk))
    out_shape = [
        jax.ShapeDtypeStruct((length, CORES * half), jnp.bfloat16),
        jax.ShapeDtypeStruct((length, CORES * half), jnp.bfloat16),
        jax.ShapeDtypeStruct((chunks * BIAS_ROWS, HD), jnp.float32),
        jax.ShapeDtypeStruct((2, length, chunks * wide), jnp.bfloat16),
    ]
    part = (CORES, 2 * HD, length) if split else (count, 2 * HD, length)
    parts = chips if split else 1
    out_shape += [jax.ShapeDtypeStruct(part, jnp.bfloat16)] * parts
    rows = CORES * length
    cols = count * length
    far = pl.BlockSpec((2, length, wide), lambda i, c: (0, 0, chunk))
    in_specs = [whole(*plan.shape), far, far]
    in_specs += [whole(*pairs[0].shape)] * len(pairs)
    operands = [plan, near_in, far_in, *pairs]
    aliases = {}
    if carried is not None:
        in_specs += [pl.BlockSpec(memory_space=pl.ANY)] * 4
        aliases = {4 + len(pairs) + k: k for k in range(4)}
        operands += list(carried)
    pack = GROUP
    while pack > 1 and pack * rows * cols > 2 * 1024 * 1024:
        pack //= 2
    grid_spec = pltpu.PrefetchScalarGridSpec(
        num_scalar_prefetch=1,
        grid=(1,),
        in_specs=in_specs,
        out_specs=[
            mine,
            mine,
            pl.BlockSpec((BIAS_ROWS, HD), lambda i, c: (chunk, 0)),
            far,
        ]
        + [whole(*part)] * parts,
        scratch_shapes=[
            pltpu.VMEM((HD, cols), jnp.bfloat16),
            pltpu.VMEM((HD, cols), jnp.bfloat16),
            pltpu.VMEM((rows, cols), jnp.float32),
            pltpu.VMEM((HD, cols), jnp.float32),
            pltpu.VMEM((HD, cols), jnp.float32),
        ]
        + [pltpu.VMEM((pack * rows, cols), jnp.float32)] * 2
        + [pltpu.VMEM((pack * rows, cols), jnp.bfloat16)] * 2
        + [
        ],
    )
    work = rows * GROUP * cols
    return pl.pallas_call(
        functools.partial(
            attention_kernel,
            carried=carried is not None,
            split=split,
            joined=len(pairs) == chips,
        ),
        grid_spec=grid_spec,
        out_shape=out_shape,
        input_output_aliases=aliases,
        compiler_params=pltpu.CompilerParams(
            vmem_limit_bytes=min(60, VMEM_MIB * cols // 1024) * 1024 * 1024
        ),
        cost_estimate=pl.CostEstimate(
            flops=12 * work * HD, transcendentals=work, bytes_accessed=8 * length * wide * 2
        ),
        name="attention",
    )(index, *operands)


def payload_kernel(index_ref, first_ref, keys, values, *outs):
    length = keys.shape[0]
    chunks = len(outs) // CORES
    index = index_ref[0]
    linked = (first_ref[0, 0] < index).astype(jnp.float32)
    flags = jnp.full((EXTRA, HD), linked, jnp.float32).astype(jnp.bfloat16)
    even = index % CORES == 0
    for hh in range(chunks):
        near, away = outs[CORES * hh : CORES * (hh + 1)]
        heads = [slice((c * chunks + hh) * HD, (c * chunks + hh + 1) * HD) for c in range(CORES)]
        for at, source in ((0, keys), (length, values)):
            first, second = source[:, heads[0]], source[:, heads[1]]
            near[at : at + length, :] = jnp.where(even, first, second)
            away[at : at + length, :] = jnp.where(even, second, first)
        near[2 * length :, :] = flags
        away[2 * length :, :] = flags


def payload(index, group_first, keys, values, chunks):
    length = keys.shape[0]
    smem = pl.BlockSpec(memory_space=pltpu.SMEM)
    vmem = pl.BlockSpec(memory_space=pltpu.VMEM)
    shape = jax.ShapeDtypeStruct((2 * length + EXTRA, HD), jnp.bfloat16)
    return pl.pallas_call(
        payload_kernel,
        in_specs=[smem, smem, vmem, vmem],
        out_shape=[shape] * (CORES * chunks),
        name="payload",
    )(index, group_first, keys, values)


def join_kernel(near, away, out):
    out[0] = near[...]
    out[1] = away[...]


def join(near, away):
    shape = jax.ShapeDtypeStruct((CORES, *near.shape), jnp.bfloat16)
    return pl.pallas_call(join_kernel, out_shape=shape, name="join")(near, away)


def place_kernel(index_ref, far, attended_in, grad_in, attended, grad_query):
    attended[...] = far[0]
    grad_query[...] = far[1]


def place(index, far, attended, grad_query):
    _, length, half = far.shape
    theirs = pl.BlockSpec((length, half), lambda i, c: (0, 1 - c[0] % CORES))
    grid_spec = pltpu.PrefetchScalarGridSpec(
        num_scalar_prefetch=1,
        grid=(1,),
        in_specs=[pl.BlockSpec((2, length, half), lambda i, c: (0, 0, 0))]
        + [pl.BlockSpec(memory_space=pl.ANY)] * 2,
        out_specs=[theirs, theirs],
    )
    return pl.pallas_call(
        place_kernel,
        grid_spec=grid_spec,
        out_shape=[jax.ShapeDtypeStruct(attended.shape, attended.dtype)] * 2,
        input_output_aliases={2: 0, 3: 1},
        compiler_params=pltpu.CompilerParams(vmem_limit_bytes=8 * 1024 * 1024),
        name="place",
    )(index, far, attended, grad_query)


def halves_kernel(index_ref, query, grad, near, away):
    half = near.shape[2]
    even = index_ref[0] % CORES == 0
    for which, source in enumerate((query, grad)):
        first, second = source[:, :half], source[:, half:]
        near[which] = jnp.where(even, first, second)
        away[which] = jnp.where(even, second, first)


def halves(index, query, grad):
    length, width = query.shape
    shape = jax.ShapeDtypeStruct((2, length, width // CORES), query.dtype)
    vmem = pl.BlockSpec(memory_space=pltpu.VMEM)
    return pl.pallas_call(
        halves_kernel,
        in_specs=[pl.BlockSpec(memory_space=pltpu.SMEM), vmem, vmem],
        out_shape=[shape, shape],
        name="halves",
    )(index, query, grad)


def added(pieces):
    total = pieces[0].astype(jnp.float32)
    for piece in pieces[1:]:
        total = total + piece.astype(jnp.float32)
    return total


def finish_kernel(index_ref, piece, *refs):
    grad_key, grad_value = refs[-2:]
    total = added([piece[z, 0] for z in range(piece.shape[0])])
    grad_key[...] = total[:HD].T.astype(jnp.bfloat16)
    grad_value[...] = total[HD:].T.astype(jnp.bfloat16)


def settle_kernel(index_ref, *refs, count):
    grad_key, grad_value, away = refs[-3:]
    total = added([piece[0] for piece in refs[:count]])
    grad_key[...] = total[:HD].T.astype(jnp.bfloat16)
    grad_value[...] = total[HD:].T.astype(jnp.bfloat16)
    away[...] = added([piece[1] for piece in refs[:count]]).astype(jnp.bfloat16)


def into_grads(kernel, index, grid, specs, operands, heads, shape, extra, carried):
    specs = list(specs)
    aliases = {}
    if carried is not None:
        specs += [pl.BlockSpec(memory_space=pl.ANY)] * 2
        aliases = {1 + len(operands): 0, 2 + len(operands): 1}
        operands = [*operands, *carried]
    block = pl.BlockSpec((shape[0], HD), heads)
    out_specs = [block, block]
    out_shape = [jax.ShapeDtypeStruct(shape, jnp.bfloat16)] * 2
    if extra is not None:
        out_specs.append(pl.BlockSpec(extra, lambda i, c: (0,) * len(extra)))
        out_shape.append(jax.ShapeDtypeStruct(extra, jnp.bfloat16))
    grid_spec = pltpu.PrefetchScalarGridSpec(
        num_scalar_prefetch=1, grid=(grid,), in_specs=specs, out_specs=out_specs
    )
    return pl.pallas_call(
        kernel,
        grid_spec=grid_spec,
        out_shape=out_shape,
        input_output_aliases=aliases,
        compiler_params=pltpu.CompilerParams(vmem_limit_bytes=8 * 1024 * 1024),
    )(index, *operands)


def finish(index, chunk, chunks, piece, shape, carried):
    count, rows, length = piece.shape
    piece = piece.reshape(count // CORES, CORES, rows, length)
    spec = pl.BlockSpec((count // CORES, 1, rows, length), lambda i, c: (0, i, 0, 0))
    heads = lambda i, c: (0, i * chunks + chunk)
    return into_grads(
        finish_kernel, index, CORES, [spec], [piece], heads, shape, None, carried
    )


def settle(index, chunk, chunks, pieces, shape, carried):
    spec = pl.BlockSpec(pieces[0].shape, lambda i, c: (0, 0, 0))
    heads = lambda i, c: (0, (c[0] % CORES) * chunks + chunk)
    kernel = functools.partial(settle_kernel, count=len(pieces))
    extra = pieces[0].shape[1:]
    return into_grads(
        kernel, index, 1, [spec] * len(pieces), pieces, heads, shape, extra, carried
    )


def receive(index, chunk, chunks, piece, shape, carried):
    piece = piece[None, None]
    spec = pl.BlockSpec(piece.shape, lambda i, c: (0, 0, 0, 0))
    heads = lambda i, c: (0, (1 - c[0] % CORES) * chunks + chunk)
    return into_grads(
        finish_kernel, index, 1, [spec], [piece], heads, shape, None, carried
    )


def bias_kernel(index_ref, sums, bias_grad, *, chunks, factor):
    core = index_ref[0] % CORES
    for c in range(CORES):
        ours = core == c
        for hh in range(chunks):
            head = c * chunks + hh
            rows = slice(hh * BIAS_ROWS, hh * BIAS_ROWS + GROUP)
            bias_grad[head * GROUP : (head + 1) * GROUP, :] = (
                jnp.where(ours, sums[0, rows, :], sums[1, rows, :]) * factor
            )
            row = slice(hh * BIAS_ROWS + GROUP, hh * BIAS_ROWS + GROUP + 1)
            at = CORES * chunks * GROUP + head
            bias_grad[at : at + 1, :] = (
                jnp.where(ours, sums[0, row, :], sums[1, row, :]) * factor
            )


def bias_total(index, sums, chunks, factor):
    return pl.pallas_call(
        functools.partial(bias_kernel, chunks=chunks, factor=factor),
        in_specs=[
            pl.BlockSpec(memory_space=pltpu.SMEM),
            pl.BlockSpec(memory_space=pltpu.VMEM),
        ],
        out_shape=jax.ShapeDtypeStruct((CORES * chunks * (GROUP + 1), HD), jnp.float32),
        compiler_params=pltpu.CompilerParams(vmem_limit_bytes=4 * 1024 * 1024),
        name="bias",
    )(index, sums)


def summed(part, axis, steps):
    size = lax.axis_size(axis)
    if len(steps) > 2:
        for step in steps:
            part = part + lax.ppermute(part, axis, [(i, i ^ step) for i in range(size)])
        return part
    total = part
    for pick in range(1, 2 ** len(steps)):
        mixed = sum(step for k, step in enumerate(steps) if pick >> k & 1)
        moved = lax.ppermute(part, axis, [(i, i ^ mixed) for i in range(size)])
        total = total + moved
    return total


def powers(start, stop):
    found = []
    while start < stop:
        found.append(start)
        start *= 2
    return found


def body(query_rows, key_rows, value_rows, out_grad, destination, group_first):
    length = query_rows.shape[0]
    devices = lax.axis_size("ctx")
    replicas = lax.axis_size("dp")
    index = lax.axis_index("ctx").astype(jnp.int32)
    kv_heads = key_rows.shape[1] // HD
    chunks = kv_heads // CORES
    plan = destination.reshape(devices, length)
    across = [(i, i ^ 1) for i in range(devices)]
    index_arg = index.reshape(1)

    chips = devices // CORES
    order = range(chips - 1, 0, -1)

    def over(k):
        return [(i, i ^ (CORES * k)) for i in range(devices)]

    def xor(r):
        return [(i, i ^ r) for i in range(devices)]

    blocks = payload(index_arg, group_first, key_rows, value_rows, chunks)
    gathered = []
    for hh in range(chunks):
        mine = blocks[CORES * hh : CORES * (hh + 1)]
        if JOIN[hh % len(JOIN)]:
            away = lax.ppermute(mine[1], "ctx", across)
            both = join(mine[0], away)
            pairs = [both] * chips
            for k in order:
                pairs[k] = lax.ppermute(both, "ctx", over(k))
        else:
            pairs = [mine[0]] * devices
            for r in range(devices - 1, 0, -1):
                pairs[r] = lax.ppermute(mine[r % CORES], "ctx", xor(r))
        gathered.append(pairs)
    near_in, far_in = halves(index_arg, query_rows, out_grad)
    far_in = lax.ppermute(far_in, "ctx", across)

    carried = None
    returned = []
    for hh in range(chunks):
        split = SPLIT[hh % len(SPLIT)]
        outs = attention(
            index_arg,
            hh,
            chunks,
            plan,
            near_in,
            far_in,
            gathered[hh],
            carried,
            split,
        )
        carried, parts = outs[:4], outs[4:]
        if split:
            pieces = list(parts)
            for k in order:
                pieces[k] = lax.ppermute(parts[k], "ctx", over(k))
            returned.append(pieces)
        else:
            returned.append(
                lax.all_to_all(parts[0], "ctx", split_axis=0, concat_axis=0, tiled=True)
            )
    attended, grad_query, bias, far_out = carried
    far_out = lax.ppermute(far_out, "ctx", across)
    attended, grad_query = place(index_arg, far_out, attended, grad_query)
    both = jnp.stack([bias, lax.ppermute(bias, "ctx", across)])
    both = summed(both, "dp", powers(1, replicas))
    both = summed(both, "ctx", powers(CORES, devices))
    factor = 1.0 / math.sqrt(length * devices * replicas)
    bias_grad = bias_total(index_arg, both, chunks, factor)
    grads = None
    shape = key_rows.shape
    for hh in range(chunks):
        if SPLIT[hh % len(SPLIT)]:
            *grads, away = settle(index_arg, hh, chunks, returned[hh], shape, grads)
            away = lax.ppermute(away, "ctx", across)
            grads = receive(index_arg, hh, chunks, away, shape, grads)
        else:
            grads = finish(index_arg, hh, chunks, returned[hh], shape, grads)
    return (attended, grad_query, *grads, bias_grad.reshape(-1))


def solution(mesh):
    rows = P(("dp", "ctx"), None)
    return jax.shard_map(
        body,
        mesh=mesh,
        in_specs=(rows, rows, rows, rows, P("dp", None), P("dp", "ctx")),
        out_specs=(rows, rows, rows, rows, P()),
        check_vma=False,
    )
```

```python
import functools
import math

import jax
import jax.numpy as jnp
from jax import lax
from jax.experimental import pallas as pl
from jax.experimental.pallas import tpu as pltpu
from jax.sharding import PartitionSpec as P


HD = 128
GROUP = 8
CORES = 2
EXTRA = 8
BIAS_ROWS = 16
NEG = -1e30
VMEM_MIB = 40
ROW_TILE = 32
JOIN = (False, True)
LOG2E = math.log2(math.e)


def nn(left, right):
    return lax.dot_general(
        left, right, (((1,), (0,)), ((), ())), preferred_element_type=jnp.float32
    )


def column(row):
    length = row.shape[1]
    down = lax.broadcasted_iota(jnp.int32, (length, length), 0)
    along = lax.broadcasted_iota(jnp.int32, (length, length), 1)
    spread = jnp.where(down == along, row.astype(jnp.float32), 0.0)
    return jnp.sum(spread, axis=1, keepdims=True).astype(jnp.int32)


def lying(upright):
    length = upright.shape[0]
    down = lax.broadcasted_iota(jnp.int32, (length, length), 0)
    along = lax.broadcasted_iota(jnp.int32, (length, length), 1)
    return jnp.sum(jnp.where(down == along, upright, 0.0), axis=0, keepdims=True)


def attention_kernel(
    index_ref, plan, query_own, grad_own, query_far, grad_far, *refs, carried, split, joined
):
    count, length = plan.shape
    chips = count // CORES
    blocks = chips if joined else count
    pairs = refs[:blocks]
    if joined:
        pairs = [p.at[j] for p in pairs for j in range(CORES)]
    refs = refs[blocks + (4 if carried else 0) :]
    attended, grad_query, bias, far_out = refs[:4]
    parts = refs[4 : 4 + (chips if split else 1)]
    key_t, value_t, mask, key_sum, value_sum, *work = refs[4 + len(parts) :]
    score_ref, press_ref, weight_ref, slope_ref = work
    pack = score_ref.shape[0] // (CORES * length)
    scaling = HD ** (-0.5)

    def gathered(start):
        return jnp.concatenate([p[start : start + length, :] for p in pairs], axis=0)

    key_t[...] = gathered(0).T
    value_t[...] = gathered(length).T
    index = index_ref[0]
    slot = jnp.concatenate(
        [column(plan[pl.ds(index, 1), :]), column(plan[pl.ds(index ^ 1, 1), :])], axis=0
    )
    block = slot // length
    reach = jnp.zeros_like(slot)
    for r in range(count):
        flag = pairs[r][2 * length : 2 * length + 1, 0:1]
        linked = (flag.astype(jnp.float32) > 0.5).astype(jnp.int32)
        reach = reach + jnp.where(block == (index ^ r), 1, 0) * linked
    first = (block - reach) * length
    for r in range(count):
        key_slot = plan[pl.ds(index ^ r, 1), :]
        mask[:, r * length : (r + 1) * length] = jnp.where(
            (key_slot <= slot) & (key_slot >= first), 0.0, NEG
        )
    key_sum[...] = jnp.zeros_like(key_sum)
    value_sum[...] = jnp.zeros_like(value_sum)
    bias[...] = jnp.zeros_like(bias)

    def pick(own, far, g):
        found = []
        for k in range(pack):
            at = pl.ds(pl.multiple_of((g + k) * HD, HD), HD)
            found += [own[:, at], far[:, at]]
        return jnp.concatenate(found, axis=0)

    def heads(j, _):
        g = j * pack
        query = pick(query_own, query_far, g)
        grad = pick(grad_own, grad_far, g)
        score_ref[...] = nn(query, key_t[...])
        press_ref[...] = nn(grad, value_t[...])
        span = CORES * length
        for r in range(0, pack * span, ROW_TILE):
            rows = slice(r, r + ROW_TILE)
            at = slice(r % span, r % span + ROW_TILE)
            score = score_ref[rows, :] * (scaling * LOG2E) + mask[at, :]
            raw = jnp.exp2(score - jnp.max(score, axis=1, keepdims=True))
            prob = raw * (1.0 / jnp.sum(raw, axis=1, keepdims=True))
            press = press_ref[rows, :]
            centred = jnp.sum(prob * press, axis=1, keepdims=True)
            weight_ref[rows, :] = prob.astype(jnp.bfloat16)
            slope_ref[rows, :] = (prob * (press - centred)).astype(jnp.bfloat16)
        weight = weight_ref[...]
        slope = slope_ref[...]
        out = nn(weight, gathered(length)).astype(jnp.bfloat16)
        into = (nn(slope, gathered(0)) * scaling).astype(jnp.bfloat16)
        for k in range(pack):
            at = pl.ds(pl.multiple_of((g + k) * HD, HD), HD)
            near = slice(k * span, k * span + length)
            away = slice(k * span + length, (k + 1) * span)
            attended[:, at] = out[near]
            grad_query[:, at] = into[near]
            far_out[0, :, at] = out[away]
            far_out[1, :, at] = into[away]
            total = jnp.sum(into[k * span : (k + 1) * span].astype(jnp.float32), axis=0)
            bias[pl.ds(g + k, 1), :] = total[None]
        key_sum[...] += nn(query.T, slope)
        value_sum[...] += nn(grad.T, weight)
        return 0

    lax.fori_loop(0, GROUP // pack, heads, 0)
    from_values = value_sum[...]
    bias[GROUP : GROUP + 1, :] = lying(jnp.sum(from_values, axis=1, keepdims=True))
    from_keys = (key_sum[...] * scaling).astype(jnp.bfloat16)
    from_values = from_values.astype(jnp.bfloat16)
    for r in range(count):
        cols = slice(r * length, (r + 1) * length)
        if split:
            parts[r // CORES][r % CORES, :HD, :] = from_keys[:, cols]
            parts[r // CORES][r % CORES, HD:, :] = from_values[:, cols]
        else:
            parts[0][index ^ r, :HD, :] = from_keys[:, cols]
            parts[0][index ^ r, HD:, :] = from_values[:, cols]


def attention(index, chunk, chunks, plan, rows_in, pairs, carried, split):
    count = plan.shape[0]
    chips = count // CORES
    length, width = rows_in[-1].shape
    wide = GROUP * HD
    whole = lambda *shape: pl.BlockSpec(shape, lambda i, c: (0,) * len(shape))
    mine = pl.BlockSpec((length, wide), lambda i, c: (0, chunks * (c[0] % CORES) + chunk))
    out_shape = [
        jax.ShapeDtypeStruct((length, width), jnp.bfloat16),
        jax.ShapeDtypeStruct((length, width), jnp.bfloat16),
        jax.ShapeDtypeStruct((chunks * BIAS_ROWS, HD), jnp.float32),
        jax.ShapeDtypeStruct((2, length, chunks * wide), jnp.bfloat16),
    ]
    part = (CORES, 2 * HD, length) if split else (count, 2 * HD, length)
    parts = chips if split else 1
    out_shape += [jax.ShapeDtypeStruct(part, jnp.bfloat16)] * parts
    rows = CORES * length
    cols = count * length
    far = pl.BlockSpec((2, length, wide), lambda i, c: (0, 0, chunk))
    near = pl.BlockSpec((length, wide), lambda i, c: (0, chunk))
    in_specs = [whole(*plan.shape), near, near, mine, mine]
    in_specs += [whole(*pairs[0].shape)] * len(pairs)
    operands = [plan, *rows_in, *pairs]
    aliases = {}
    if carried is not None:
        in_specs += [pl.BlockSpec(memory_space=pl.ANY)] * 4
        aliases = {6 + len(pairs) + k: k for k in range(4)}
        operands += list(carried)
    pack = GROUP
    while pack > 1 and pack * rows * cols > 2 * 1024 * 1024:
        pack //= 2
    grid_spec = pltpu.PrefetchScalarGridSpec(
        num_scalar_prefetch=1,
        grid=(1,),
        in_specs=in_specs,
        out_specs=[
            mine,
            mine,
            pl.BlockSpec((BIAS_ROWS, HD), lambda i, c: (chunk, 0)),
            far,
        ]
        + [whole(*part)] * parts,
        scratch_shapes=[
            pltpu.VMEM((HD, cols), jnp.bfloat16),
            pltpu.VMEM((HD, cols), jnp.bfloat16),
            pltpu.VMEM((rows, cols), jnp.float32),
            pltpu.VMEM((HD, cols), jnp.float32),
            pltpu.VMEM((HD, cols), jnp.float32),
        ]
        + [pltpu.VMEM((pack * rows, cols), jnp.float32)] * 2
        + [pltpu.VMEM((pack * rows, cols), jnp.bfloat16)] * 2
        + [],
    )
    work = rows * GROUP * cols
    return pl.pallas_call(
        functools.partial(
            attention_kernel,
            carried=carried is not None,
            split=split,
            joined=len(pairs) == chips,
        ),
        grid_spec=grid_spec,
        out_shape=out_shape,
        input_output_aliases=aliases,
        compiler_params=pltpu.CompilerParams(
            vmem_limit_bytes=min(60, VMEM_MIB * cols // 1024) * 1024 * 1024
        ),
        cost_estimate=pl.CostEstimate(
            flops=12 * work * HD, transcendentals=work, bytes_accessed=8 * length * wide * 2
        ),
        name="attention",
    )(index, *operands)


def payload_kernel(index_ref, first_ref, keys, values, *outs):
    length = keys.shape[0]
    chunks = len(outs) // CORES
    index = index_ref[0]
    linked = (first_ref[0, 0] < index).astype(jnp.float32)
    flags = jnp.full((EXTRA, HD), linked, jnp.float32).astype(jnp.bfloat16)
    even = index % CORES == 0
    for hh in range(chunks):
        near, away = outs[CORES * hh : CORES * (hh + 1)]
        heads = [slice((c * chunks + hh) * HD, (c * chunks + hh + 1) * HD) for c in range(CORES)]
        for at, source in ((0, keys), (length, values)):
            first, second = source[:, heads[0]], source[:, heads[1]]
            near[at : at + length, :] = jnp.where(even, first, second)
            away[at : at + length, :] = jnp.where(even, second, first)
        near[2 * length :, :] = flags
        away[2 * length :, :] = flags


def payload(index, group_first, keys, values, chunks):
    length = keys.shape[0]
    smem = pl.BlockSpec(memory_space=pltpu.SMEM)
    vmem = pl.BlockSpec(memory_space=pltpu.VMEM)
    shape = jax.ShapeDtypeStruct((2 * length + EXTRA, HD), jnp.bfloat16)
    return pl.pallas_call(
        payload_kernel,
        in_specs=[smem, smem, vmem, vmem],
        out_shape=[shape] * (CORES * chunks),
        name="payload",
    )(index, group_first, keys, values)


def join_kernel(near, away, out):
    out[0] = near[...]
    out[1] = away[...]


def join(near, away):
    shape = jax.ShapeDtypeStruct((CORES, *near.shape), jnp.bfloat16)
    return pl.pallas_call(join_kernel, out_shape=shape, name="join")(near, away)


def place_kernel(index_ref, far, piece, *refs):
    attended, grad_query, grad_key, grad_value = refs[-4:]
    attended[...] = far[0]
    grad_query[...] = far[1]
    grad_key[...] = piece[:HD].astype(jnp.float32).T.astype(jnp.bfloat16)
    grad_value[...] = piece[HD:].astype(jnp.float32).T.astype(jnp.bfloat16)


def place(index, chunk, chunks, far, piece, filled):
    _, length, half = far.shape
    theirs = pl.BlockSpec((length, half), lambda i, c: (0, 1 - c[0] % CORES))
    head = pl.BlockSpec((length, HD), lambda i, c: (0, (1 - c[0] % CORES) * chunks + chunk))
    grid_spec = pltpu.PrefetchScalarGridSpec(
        num_scalar_prefetch=1,
        grid=(1,),
        in_specs=[
            pl.BlockSpec(far.shape, lambda i, c: (0, 0, 0)),
            pl.BlockSpec(piece.shape, lambda i, c: (0, 0)),
        ]
        + [pl.BlockSpec(memory_space=pl.ANY)] * 4,
        out_specs=[theirs, theirs, head, head],
    )
    return pl.pallas_call(
        place_kernel,
        grid_spec=grid_spec,
        out_shape=[jax.ShapeDtypeStruct(x.shape, x.dtype) for x in filled],
        input_output_aliases={3 + k: k for k in range(4)},
        compiler_params=pltpu.CompilerParams(vmem_limit_bytes=8 * 1024 * 1024),
        name="place",
    )(index, far, piece, *filled)


def added(pieces):
    total = pieces[0].astype(jnp.float32)
    for piece in pieces[1:]:
        total = total + piece.astype(jnp.float32)
    return total


def settle_kernel(index_ref, *refs, count):
    grad_key, grad_value, away = refs[-3:]
    total = added([piece[0] for piece in refs[:count]])
    grad_key[...] = total[:HD].T.astype(jnp.bfloat16)
    grad_value[...] = total[HD:].T.astype(jnp.bfloat16)
    away[...] = added([piece[1] for piece in refs[:count]]).astype(jnp.bfloat16)


def into_grads(kernel, index, grid, specs, operands, heads, shape, extra, carried):
    specs = list(specs)
    aliases = {}
    if carried is not None:
        specs += [pl.BlockSpec(memory_space=pl.ANY)] * 2
        aliases = {1 + len(operands): 0, 2 + len(operands): 1}
        operands = [*operands, *carried]
    block = pl.BlockSpec((shape[0], HD), heads)
    out_specs = [block, block]
    out_shape = [jax.ShapeDtypeStruct(shape, jnp.bfloat16)] * 2
    if extra is not None:
        out_specs.append(pl.BlockSpec(extra, lambda i, c: (0,) * len(extra)))
        out_shape.append(jax.ShapeDtypeStruct(extra, jnp.bfloat16))
    grid_spec = pltpu.PrefetchScalarGridSpec(
        num_scalar_prefetch=1, grid=(grid,), in_specs=specs, out_specs=out_specs
    )
    return pl.pallas_call(
        kernel,
        grid_spec=grid_spec,
        out_shape=out_shape,
        input_output_aliases=aliases,
        compiler_params=pltpu.CompilerParams(vmem_limit_bytes=8 * 1024 * 1024),
    )(index, *operands)


def settle(index, chunk, chunks, pieces, shape, carried):
    spec = pl.BlockSpec(pieces[0].shape, lambda i, c: (0, 0, 0))
    heads = lambda i, c: (0, (c[0] % CORES) * chunks + chunk)
    kernel = functools.partial(settle_kernel, count=len(pieces))
    extra = pieces[0].shape[1:]
    return into_grads(kernel, index, 1, [spec] * len(pieces), pieces, heads, shape, extra, carried)


def last_kernel(index_ref, sums, piece, *refs, chunks, factor):
    grad_key, grad_value, bias_grad = refs[-3:]
    grad_key[...] = piece[:HD].astype(jnp.float32).T.astype(jnp.bfloat16)
    grad_value[...] = piece[HD:].astype(jnp.float32).T.astype(jnp.bfloat16)
    core = index_ref[0] % CORES
    for c in range(CORES):
        ours = core == c
        for hh in range(chunks):
            head = c * chunks + hh
            rows = slice(hh * BIAS_ROWS, hh * BIAS_ROWS + GROUP)
            bias_grad[head * GROUP : (head + 1) * GROUP, :] = (
                jnp.where(ours, sums[0, rows, :], sums[1, rows, :]) * factor
            )
            row = slice(hh * BIAS_ROWS + GROUP, hh * BIAS_ROWS + GROUP + 1)
            at = CORES * chunks * GROUP + head
            bias_grad[at : at + 1, :] = (
                jnp.where(ours, sums[0, row, :], sums[1, row, :]) * factor
            )


def last(index, sums, chunk, chunks, piece, grads, factor):
    length = grads[0].shape[0]
    head = pl.BlockSpec((length, HD), lambda i, c: (0, (1 - c[0] % CORES) * chunks + chunk))
    bias_shape = (CORES * chunks * (GROUP + 1), HD)
    grid_spec = pltpu.PrefetchScalarGridSpec(
        num_scalar_prefetch=1,
        grid=(1,),
        in_specs=[
            pl.BlockSpec(sums.shape, lambda i, c: (0, 0, 0)),
            pl.BlockSpec(piece.shape, lambda i, c: (0, 0)),
        ]
        + [pl.BlockSpec(memory_space=pl.ANY)] * 2,
        out_specs=[head, head, pl.BlockSpec(bias_shape, lambda i, c: (0, 0))],
    )
    return pl.pallas_call(
        functools.partial(last_kernel, chunks=chunks, factor=factor),
        grid_spec=grid_spec,
        out_shape=[jax.ShapeDtypeStruct(x.shape, x.dtype) for x in grads]
        + [jax.ShapeDtypeStruct(bias_shape, jnp.float32)],
        input_output_aliases={3: 0, 4: 1},
        compiler_params=pltpu.CompilerParams(vmem_limit_bytes=8 * 1024 * 1024),
        name="last",
    )(index, sums, piece, *grads)


def summed(part, axis, steps):
    size = lax.axis_size(axis)
    if len(steps) > 2:
        for step in steps:
            part = part + lax.ppermute(part, axis, [(i, i ^ step) for i in range(size)])
        return part
    total = part
    for pick in range(1, 2 ** len(steps)):
        mixed = sum(step for k, step in enumerate(steps) if pick >> k & 1)
        moved = lax.ppermute(part, axis, [(i, i ^ mixed) for i in range(size)])
        total = total + moved
    return total


def powers(start, stop):
    found = []
    while start < stop:
        found.append(start)
        start *= 2
    return found


def body(query_rows, key_rows, value_rows, out_grad, destination, group_first):
    length = query_rows.shape[0]
    devices = lax.axis_size("ctx")
    replicas = lax.axis_size("dp")
    index = lax.axis_index("ctx").astype(jnp.int32)
    kv_heads = key_rows.shape[1] // HD
    chunks = kv_heads // CORES
    plan = destination.reshape(devices, length)
    across = [(i, i ^ 1) for i in range(devices)]
    index_arg = index.reshape(1)

    chips = devices // CORES
    order = range(chips - 1, 0, -1)

    def over(k):
        return [(i, i ^ (CORES * k)) for i in range(devices)]

    def xor(r):
        return [(i, i ^ r) for i in range(devices)]

    query_far = lax.ppermute(query_rows, "ctx", across)
    grad_far = lax.ppermute(out_grad, "ctx", across)
    half = query_rows.shape[1] // CORES
    begin = (index % CORES) * half
    near = [lax.dynamic_slice_in_dim(rows, begin, half, axis=1) for rows in (query_rows, out_grad)]
    rows_in = (*near, query_far, grad_far)
    blocks = payload(index_arg, group_first, key_rows, value_rows, chunks)
    gathered = []
    for hh in range(chunks):
        mine = blocks[CORES * hh : CORES * (hh + 1)]
        if JOIN[hh % len(JOIN)]:
            away = lax.ppermute(mine[1], "ctx", across)
            both = join(mine[0], away)
            pairs = [both] * chips
            for k in order:
                pairs[k] = lax.ppermute(both, "ctx", over(k))
        else:
            pairs = [mine[0]] * devices
            for r in range(devices - 1, 0, -1):
                pairs[r] = lax.ppermute(mine[r % CORES], "ctx", xor(r))
        gathered.append(pairs)
    carried = None
    returned = []
    for hh in range(chunks):
        outs = attention(
            index_arg,
            hh,
            chunks,
            plan,
            rows_in,
            gathered[hh],
            carried,
            True,
        )
        carried, parts = outs[:4], outs[4:]
        pieces = list(parts)
        for k in order:
            pieces[k] = lax.ppermute(parts[k], "ctx", over(k))
        returned.append(pieces)
    attended, grad_query, bias, far_out = carried
    far_out = lax.ppermute(far_out, "ctx", across)
    both = jnp.stack([bias, lax.ppermute(bias, "ctx", across)])
    both = summed(both, "dp", powers(1, replicas))
    both = summed(both, "ctx", powers(CORES, devices))
    factor = 1.0 / math.sqrt(length * devices * replicas)
    grads = None
    for hh in range(chunks):
        *grads, away = settle(index_arg, hh, chunks, returned[hh], key_rows.shape, grads)
        away = lax.ppermute(away, "ctx", across)
        if hh < chunks - 1:
            attended, grad_query, *grads = place(
                index_arg, hh, chunks, far_out, away, (attended, grad_query, *grads)
            )
    *grads, bias_grad = last(index_arg, both, chunks - 1, chunks, away, grads, factor)
    return (attended, grad_query, *grads, bias_grad.reshape(-1))


def solution(mesh):
    rows = P(("dp", "ctx"), None)
    return jax.shard_map(
        body,
        mesh=mesh,
        in_specs=(rows, rows, rows, rows, P("dp", None), P("dp", "ctx")),
        out_specs=(rows, rows, rows, rows, P()),
        check_vma=False,
    )
```

```python
import functools
import math

import jax
import jax.numpy as jnp
from jax import lax
from jax.experimental import pallas as pl
from jax.experimental.pallas import tpu as pltpu
from jax.sharding import PartitionSpec as P


HD = 128
GROUP = 8
CORES = 2
EXTRA = 8
BIAS_ROWS = 16
NEG = -1e30
VMEM_MIB = 40
ROW_TILE = 32
JOIN = (False, True)
LOG2E = math.log2(math.e)


def nn(left, right):
    return lax.dot_general(
        left, right, (((1,), (0,)), ((), ())), preferred_element_type=jnp.float32
    )


def column(row):
    length = row.shape[1]
    down = lax.broadcasted_iota(jnp.int32, (length, length), 0)
    along = lax.broadcasted_iota(jnp.int32, (length, length), 1)
    spread = jnp.where(down == along, row.astype(jnp.float32), 0.0)
    return jnp.sum(spread, axis=1, keepdims=True).astype(jnp.int32)


def lying(upright):
    length = upright.shape[0]
    down = lax.broadcasted_iota(jnp.int32, (length, length), 0)
    along = lax.broadcasted_iota(jnp.int32, (length, length), 1)
    return jnp.sum(jnp.where(down == along, upright, 0.0), axis=0, keepdims=True)


def attention_kernel(
    index_ref, plan, query_own, grad_own, query_far, grad_far, *refs, carried, split, joined
):
    count, length = plan.shape
    chips = count // CORES
    blocks = chips if joined else count
    pairs = refs[:blocks]
    if joined:
        pairs = [p.at[j] for p in pairs for j in range(CORES)]
    refs = refs[blocks + (4 if carried else 0) :]
    attended, grad_query, bias, far_out = refs[:4]
    parts = refs[4 : 4 + (chips if split else 1)]
    key_t, value_t, mask, key_sum, value_sum, *work = refs[4 + len(parts) :]
    score_ref, press_ref, weight_ref, slope_ref = work
    pack = score_ref.shape[0] // (CORES * length)
    scaling = HD ** (-0.5)

    def gathered(start):
        return jnp.concatenate([p[start : start + length, :] for p in pairs], axis=0)

    key_t[...] = gathered(0).T
    value_t[...] = gathered(length).T
    index = index_ref[0]
    slot = jnp.concatenate(
        [column(plan[pl.ds(index, 1), :]), column(plan[pl.ds(index ^ 1, 1), :])], axis=0
    )
    block = slot // length
    reach = jnp.zeros_like(slot)
    for r in range(count):
        flag = pairs[r][2 * length : 2 * length + 1, 0:1]
        linked = (flag.astype(jnp.float32) > 0.5).astype(jnp.int32)
        reach = reach + jnp.where(block == (index ^ r), 1, 0) * linked
    first = (block - reach) * length
    for r in range(count):
        key_slot = plan[pl.ds(index ^ r, 1), :]
        mask[:, r * length : (r + 1) * length] = jnp.where(
            (key_slot <= slot) & (key_slot >= first), 0.0, NEG
        )
    key_sum[...] = jnp.zeros_like(key_sum)
    value_sum[...] = jnp.zeros_like(value_sum)
    bias[...] = jnp.zeros_like(bias)

    def pick(own, far, g):
        found = []
        for k in range(pack):
            at = pl.ds(pl.multiple_of((g + k) * HD, HD), HD)
            found += [own[:, at], far[:, at]]
        return jnp.concatenate(found, axis=0)

    def heads(j, _):
        g = j * pack
        query = pick(query_own, query_far, g)
        grad = pick(grad_own, grad_far, g)
        score_ref[...] = nn(query, key_t[...])
        press_ref[...] = nn(grad, value_t[...])
        span = CORES * length
        for r in range(0, pack * span, ROW_TILE):
            rows = slice(r, r + ROW_TILE)
            at = slice(r % span, r % span + ROW_TILE)
            score = score_ref[rows, :] * (scaling * LOG2E) + mask[at, :]
            raw = jnp.exp2(score - jnp.max(score, axis=1, keepdims=True))
            prob = raw * (1.0 / jnp.sum(raw, axis=1, keepdims=True))
            press = press_ref[rows, :]
            centred = jnp.sum(prob * press, axis=1, keepdims=True)
            weight_ref[rows, :] = prob.astype(jnp.bfloat16)
            slope_ref[rows, :] = (prob * (press - centred)).astype(jnp.bfloat16)
        weight = weight_ref[...]
        slope = slope_ref[...]
        out = nn(weight, gathered(length)).astype(jnp.bfloat16)
        into = (nn(slope, gathered(0)) * scaling).astype(jnp.bfloat16)
        for k in range(pack):
            at = pl.ds(pl.multiple_of((g + k) * HD, HD), HD)
            near = slice(k * span, k * span + length)
            away = slice(k * span + length, (k + 1) * span)
            attended[:, at] = out[near]
            grad_query[:, at] = into[near]
            far_out[0, :, at] = out[away]
            far_out[1, :, at] = into[away]
            total = jnp.sum(into[k * span : (k + 1) * span].astype(jnp.float32), axis=0)
            bias[pl.ds(g + k, 1), :] = total[None]
        key_sum[...] += nn(query.T, slope)
        value_sum[...] += nn(grad.T, weight)
        return 0

    lax.fori_loop(0, GROUP // pack, heads, 0)
    from_values = value_sum[...]
    bias[GROUP : GROUP + 1, :] = lying(jnp.sum(from_values, axis=1, keepdims=True))
    from_keys = (key_sum[...] * scaling).astype(jnp.bfloat16)
    from_values = from_values.astype(jnp.bfloat16)
    for r in range(count):
        cols = slice(r * length, (r + 1) * length)
        if split:
            parts[r // CORES][r % CORES, :HD, :] = from_keys[:, cols]
            parts[r // CORES][r % CORES, HD:, :] = from_values[:, cols]
        else:
            parts[0][index ^ r, :HD, :] = from_keys[:, cols]
            parts[0][index ^ r, HD:, :] = from_values[:, cols]


def attention(index, chunk, chunks, plan, rows_in, pairs, carried, split):
    count = plan.shape[0]
    chips = count // CORES
    length, width = rows_in[-1].shape
    wide = GROUP * HD
    whole = lambda *shape: pl.BlockSpec(shape, lambda i, c: (0,) * len(shape))
    mine = pl.BlockSpec((length, wide), lambda i, c: (0, chunks * (c[0] % CORES) + chunk))
    out_shape = [
        jax.ShapeDtypeStruct((length, width), jnp.bfloat16),
        jax.ShapeDtypeStruct((length, width), jnp.bfloat16),
        jax.ShapeDtypeStruct((chunks * BIAS_ROWS, HD), jnp.float32),
        jax.ShapeDtypeStruct((2, length, chunks * wide), jnp.bfloat16),
    ]
    part = (CORES, 2 * HD, length) if split else (count, 2 * HD, length)
    parts = chips if split else 1
    out_shape += [jax.ShapeDtypeStruct(part, jnp.bfloat16)] * parts
    rows = CORES * length
    cols = count * length
    far = pl.BlockSpec((2, length, wide), lambda i, c: (0, 0, chunk))
    near = pl.BlockSpec((length, wide), lambda i, c: (0, chunk))
    in_specs = [whole(*plan.shape), near, near, mine, mine]
    in_specs += [whole(*pairs[0].shape)] * len(pairs)
    operands = [plan, *rows_in, *pairs]
    aliases = {}
    if carried is not None:
        in_specs += [pl.BlockSpec(memory_space=pl.ANY)] * 4
        aliases = {6 + len(pairs) + k: k for k in range(4)}
        operands += list(carried)
    pack = GROUP
    while pack > 1 and pack * rows * cols > 2 * 1024 * 1024:
        pack //= 2
    grid_spec = pltpu.PrefetchScalarGridSpec(
        num_scalar_prefetch=1,
        grid=(1,),
        in_specs=in_specs,
        out_specs=[
            mine,
            mine,
            pl.BlockSpec((BIAS_ROWS, HD), lambda i, c: (chunk, 0)),
            far,
        ]
        + [whole(*part)] * parts,
        scratch_shapes=[
            pltpu.VMEM((HD, cols), jnp.bfloat16),
            pltpu.VMEM((HD, cols), jnp.bfloat16),
            pltpu.VMEM((rows, cols), jnp.float32),
            pltpu.VMEM((HD, cols), jnp.float32),
            pltpu.VMEM((HD, cols), jnp.float32),
        ]
        + [pltpu.VMEM((pack * rows, cols), jnp.float32)] * 2
        + [pltpu.VMEM((pack * rows, cols), jnp.bfloat16)] * 2
        + [],
    )
    work = rows * GROUP * cols
    return pl.pallas_call(
        functools.partial(
            attention_kernel,
            carried=carried is not None,
            split=split,
            joined=len(pairs) == chips,
        ),
        grid_spec=grid_spec,
        out_shape=out_shape,
        input_output_aliases=aliases,
        compiler_params=pltpu.CompilerParams(
            vmem_limit_bytes=min(60, VMEM_MIB * cols // 1024) * 1024 * 1024
        ),
        cost_estimate=pl.CostEstimate(
            flops=12 * work * HD, transcendentals=work, bytes_accessed=8 * length * wide * 2
        ),
        name="attention",
    )(index, *operands)


def payload_kernel(index_ref, first_ref, keys, values, *outs):
    length = keys.shape[0]
    chunks = len(outs) // CORES
    index = index_ref[0]
    linked = (first_ref[0, 0] < index).astype(jnp.float32)
    flags = jnp.full((EXTRA, HD), linked, jnp.float32).astype(jnp.bfloat16)
    even = index % CORES == 0
    for hh in range(chunks):
        near, away = outs[CORES * hh : CORES * (hh + 1)]
        heads = [slice((c * chunks + hh) * HD, (c * chunks + hh + 1) * HD) for c in range(CORES)]
        for at, source in ((0, keys), (length, values)):
            first, second = source[:, heads[0]], source[:, heads[1]]
            near[at : at + length, :] = jnp.where(even, first, second)
            away[at : at + length, :] = jnp.where(even, second, first)
        near[2 * length :, :] = flags
        away[2 * length :, :] = flags


def payload(index, group_first, keys, values, chunks):
    length = keys.shape[0]
    smem = pl.BlockSpec(memory_space=pltpu.SMEM)
    vmem = pl.BlockSpec(memory_space=pltpu.VMEM)
    shape = jax.ShapeDtypeStruct((2 * length + EXTRA, HD), jnp.bfloat16)
    return pl.pallas_call(
        payload_kernel,
        in_specs=[smem, smem, vmem, vmem],
        out_shape=[shape] * (CORES * chunks),
        name="payload",
    )(index, group_first, keys, values)


def place_kernel(index_ref, far, piece, *refs):
    attended, grad_query, grad_key, grad_value = refs[-4:]
    attended[...] = far[0]
    grad_query[...] = far[1]
    grad_key[...] = piece[:HD].astype(jnp.float32).T.astype(jnp.bfloat16)
    grad_value[...] = piece[HD:].astype(jnp.float32).T.astype(jnp.bfloat16)


def place(index, chunk, chunks, far, piece, filled):
    _, length, half = far.shape
    theirs = pl.BlockSpec((length, half), lambda i, c: (0, 1 - c[0] % CORES))
    head = pl.BlockSpec((length, HD), lambda i, c: (0, (1 - c[0] % CORES) * chunks + chunk))
    grid_spec = pltpu.PrefetchScalarGridSpec(
        num_scalar_prefetch=1,
        grid=(1,),
        in_specs=[
            pl.BlockSpec(far.shape, lambda i, c: (0, 0, 0)),
            pl.BlockSpec(piece.shape, lambda i, c: (0, 0)),
        ]
        + [pl.BlockSpec(memory_space=pl.ANY)] * 4,
        out_specs=[theirs, theirs, head, head],
    )
    return pl.pallas_call(
        place_kernel,
        grid_spec=grid_spec,
        out_shape=[jax.ShapeDtypeStruct(x.shape, x.dtype) for x in filled],
        input_output_aliases={3 + k: k for k in range(4)},
        compiler_params=pltpu.CompilerParams(vmem_limit_bytes=8 * 1024 * 1024),
        name="place",
    )(index, far, piece, *filled)


def added(pieces):
    total = pieces[0].astype(jnp.float32)
    for piece in pieces[1:]:
        total = total + piece.astype(jnp.float32)
    return total


def settle_kernel(index_ref, *refs, count):
    grad_key, grad_value, away = refs[-3:]
    total = added([piece[0] for piece in refs[:count]])
    grad_key[...] = total[:HD].T.astype(jnp.bfloat16)
    grad_value[...] = total[HD:].T.astype(jnp.bfloat16)
    away[...] = added([piece[1] for piece in refs[:count]]).astype(jnp.bfloat16)


def into_grads(kernel, index, grid, specs, operands, heads, shape, extra, carried):
    specs = list(specs)
    aliases = {}
    if carried is not None:
        specs += [pl.BlockSpec(memory_space=pl.ANY)] * 2
        aliases = {1 + len(operands): 0, 2 + len(operands): 1}
        operands = [*operands, *carried]
    block = pl.BlockSpec((shape[0], HD), heads)
    out_specs = [block, block]
    out_shape = [jax.ShapeDtypeStruct(shape, jnp.bfloat16)] * 2
    if extra is not None:
        out_specs.append(pl.BlockSpec(extra, lambda i, c: (0,) * len(extra)))
        out_shape.append(jax.ShapeDtypeStruct(extra, jnp.bfloat16))
    grid_spec = pltpu.PrefetchScalarGridSpec(
        num_scalar_prefetch=1, grid=(grid,), in_specs=specs, out_specs=out_specs
    )
    return pl.pallas_call(
        kernel,
        grid_spec=grid_spec,
        out_shape=out_shape,
        input_output_aliases=aliases,
        compiler_params=pltpu.CompilerParams(vmem_limit_bytes=8 * 1024 * 1024),
    )(index, *operands)


def settle(index, chunk, chunks, pieces, shape, carried):
    spec = pl.BlockSpec(pieces[0].shape, lambda i, c: (0, 0, 0))
    heads = lambda i, c: (0, (c[0] % CORES) * chunks + chunk)
    kernel = functools.partial(settle_kernel, count=len(pieces))
    extra = pieces[0].shape[1:]
    return into_grads(kernel, index, 1, [spec] * len(pieces), pieces, heads, shape, extra, carried)


def last_kernel(index_ref, sums, piece, *refs, chunks, factor):
    grad_key, grad_value, bias_grad = refs[-3:]
    grad_key[...] = piece[:HD].astype(jnp.float32).T.astype(jnp.bfloat16)
    grad_value[...] = piece[HD:].astype(jnp.float32).T.astype(jnp.bfloat16)
    core = index_ref[0] % CORES
    for c in range(CORES):
        ours = core == c
        for hh in range(chunks):
            head = c * chunks + hh
            rows = slice(hh * BIAS_ROWS, hh * BIAS_ROWS + GROUP)
            bias_grad[head * GROUP : (head + 1) * GROUP, :] = (
                jnp.where(ours, sums[0, rows, :], sums[1, rows, :]) * factor
            )
            row = slice(hh * BIAS_ROWS + GROUP, hh * BIAS_ROWS + GROUP + 1)
            at = CORES * chunks * GROUP + head
            bias_grad[at : at + 1, :] = (
                jnp.where(ours, sums[0, row, :], sums[1, row, :]) * factor
            )


def last(index, sums, chunk, chunks, piece, grads, factor):
    length = grads[0].shape[0]
    head = pl.BlockSpec((length, HD), lambda i, c: (0, (1 - c[0] % CORES) * chunks + chunk))
    bias_shape = (CORES * chunks * (GROUP + 1), HD)
    grid_spec = pltpu.PrefetchScalarGridSpec(
        num_scalar_prefetch=1,
        grid=(1,),
        in_specs=[
            pl.BlockSpec(sums.shape, lambda i, c: (0, 0, 0)),
            pl.BlockSpec(piece.shape, lambda i, c: (0, 0)),
        ]
        + [pl.BlockSpec(memory_space=pl.ANY)] * 2,
        out_specs=[head, head, pl.BlockSpec(bias_shape, lambda i, c: (0, 0))],
    )
    return pl.pallas_call(
        functools.partial(last_kernel, chunks=chunks, factor=factor),
        grid_spec=grid_spec,
        out_shape=[jax.ShapeDtypeStruct(x.shape, x.dtype) for x in grads]
        + [jax.ShapeDtypeStruct(bias_shape, jnp.float32)],
        input_output_aliases={3: 0, 4: 1},
        compiler_params=pltpu.CompilerParams(vmem_limit_bytes=8 * 1024 * 1024),
        name="last",
    )(index, sums, piece, *grads)


def summed(part, axis, steps):
    size = lax.axis_size(axis)
    if len(steps) > 2:
        for step in steps:
            part = part + lax.ppermute(part, axis, [(i, i ^ step) for i in range(size)])
        return part
    total = part
    for pick in range(1, 2 ** len(steps)):
        mixed = sum(step for k, step in enumerate(steps) if pick >> k & 1)
        moved = lax.ppermute(part, axis, [(i, i ^ mixed) for i in range(size)])
        total = total + moved
    return total


def powers(start, stop):
    found = []
    while start < stop:
        found.append(start)
        start *= 2
    return found


def body(query_rows, key_rows, value_rows, out_grad, destination, group_first):
    length = query_rows.shape[0]
    devices = lax.axis_size("ctx")
    replicas = lax.axis_size("dp")
    index = lax.axis_index("ctx").astype(jnp.int32)
    kv_heads = key_rows.shape[1] // HD
    chunks = kv_heads // CORES
    plan = destination.reshape(devices, length)
    across = [(i, i ^ 1) for i in range(devices)]
    index_arg = index.reshape(1)

    chips = devices // CORES
    order = range(chips - 1, 0, -1)

    def over(k):
        return [(i, i ^ (CORES * k)) for i in range(devices)]

    def xor(r):
        return [(i, i ^ r) for i in range(devices)]

    query_far = lax.ppermute(query_rows, "ctx", across)
    grad_far = lax.ppermute(out_grad, "ctx", across)
    half = query_rows.shape[1] // CORES
    begin = (index % CORES) * half
    near = [lax.dynamic_slice_in_dim(rows, begin, half, axis=1) for rows in (query_rows, out_grad)]
    rows_in = (*near, query_far, grad_far)
    blocks = payload(index_arg, group_first, key_rows, value_rows, chunks)
    gathered = []
    for hh in range(chunks):
        mine = blocks[CORES * hh : CORES * (hh + 1)]
        if JOIN[hh % len(JOIN)]:
            away = lax.ppermute(mine[1], "ctx", across)
            both = jnp.stack([mine[0], away])
            pairs = [both] * chips
            for k in order:
                pairs[k] = lax.ppermute(both, "ctx", over(k))
        else:
            pairs = [mine[0]] * devices
            for r in range(devices - 1, 0, -1):
                pairs[r] = lax.ppermute(mine[r % CORES], "ctx", xor(r))
        gathered.append(pairs)
    carried = None
    returned = []
    for hh in range(chunks):
        outs = attention(
            index_arg,
            hh,
            chunks,
            plan,
            rows_in,
            gathered[hh],
            carried,
            True,
        )
        carried, parts = outs[:4], outs[4:]
        pieces = list(parts)
        for k in order:
            pieces[k] = lax.ppermute(parts[k], "ctx", over(k))
        returned.append(pieces)
    attended, grad_query, bias, far_out = carried
    far_out = lax.ppermute(far_out, "ctx", across)
    both = jnp.stack([bias, lax.ppermute(bias, "ctx", across)])
    both = summed(both, "dp", powers(1, replicas))
    both = summed(both, "ctx", powers(CORES, devices))
    factor = 1.0 / math.sqrt(length * devices * replicas)
    grads = None
    for hh in range(chunks):
        *grads, away = settle(index_arg, hh, chunks, returned[hh], key_rows.shape, grads)
        away = lax.ppermute(away, "ctx", across)
        if hh < chunks - 1:
            attended, grad_query, *grads = place(
                index_arg, hh, chunks, far_out, away, (attended, grad_query, *grads)
            )
    *grads, bias_grad = last(index_arg, both, chunks - 1, chunks, away, grads, factor)
    return (attended, grad_query, *grads, bias_grad.reshape(-1))


def solution(mesh):
    rows = P(("dp", "ctx"), None)
    return jax.shard_map(
        body,
        mesh=mesh,
        in_specs=(rows, rows, rows, rows, P("dp", None), P("dp", "ctx")),
        out_specs=(rows, rows, rows, rows, P()),
        check_vma=False,
    )
```

```python
import functools
import math

import jax
import jax.numpy as jnp
from jax import lax
from jax.experimental import pallas as pl
from jax.experimental.pallas import tpu as pltpu
from jax.sharding import PartitionSpec as P


HD = 128
GROUP = 8
CORES = 2
EXTRA = 8
BIAS_ROWS = 16
NEG = -1e30
VMEM_MIB = 40
ROW_TILE = 32
JOIN = (False, True)
LOG2E = math.log2(math.e)


def nn(left, right):
    return lax.dot_general(
        left, right, (((1,), (0,)), ((), ())), preferred_element_type=jnp.float32
    )


def column(row):
    length = row.shape[1]
    down = lax.broadcasted_iota(jnp.int32, (length, length), 0)
    along = lax.broadcasted_iota(jnp.int32, (length, length), 1)
    spread = jnp.where(down == along, row.astype(jnp.float32), 0.0)
    return jnp.sum(spread, axis=1, keepdims=True).astype(jnp.int32)


def lying(upright):
    length = upright.shape[0]
    down = lax.broadcasted_iota(jnp.int32, (length, length), 0)
    along = lax.broadcasted_iota(jnp.int32, (length, length), 1)
    return jnp.sum(jnp.where(down == along, upright, 0.0), axis=0, keepdims=True)


def attention_kernel(
    index_ref, plan, query_own, grad_own, query_far, grad_far, *refs, carried, split, joined
):
    count, length = plan.shape
    chips = count // CORES
    blocks = chips if joined else count
    pairs = refs[:blocks]
    if joined:
        pairs = [p.at[j] for p in pairs for j in range(CORES)]
    refs = refs[blocks + (4 if carried else 0) :]
    attended, grad_query, bias, far_out = refs[:4]
    parts = refs[4 : 4 + (chips if split else 1)]
    key_t, value_t, mask, key_sum, value_sum, *work = refs[4 + len(parts) :]
    score_ref, press_ref, weight_ref, slope_ref = work
    pack = score_ref.shape[0] // (CORES * length)
    scaling = HD ** (-0.5)

    def gathered(start):
        return jnp.concatenate([p[start : start + length, :] for p in pairs], axis=0)

    key_t[...] = gathered(0).T
    value_t[...] = gathered(length).T
    index = index_ref[0]
    slot = jnp.concatenate(
        [column(plan[pl.ds(index, 1), :]), column(plan[pl.ds(index ^ 1, 1), :])], axis=0
    )
    block = slot // length
    reach = jnp.zeros_like(slot)
    for r in range(count):
        flag = pairs[r][2 * length : 2 * length + 1, 0:1]
        linked = (flag.astype(jnp.float32) > 0.5).astype(jnp.int32)
        reach = reach + jnp.where(block == (index ^ r), 1, 0) * linked
    first = (block - reach) * length
    for r in range(count):
        key_slot = plan[pl.ds(index ^ r, 1), :]
        mask[:, r * length : (r + 1) * length] = jnp.where(
            (key_slot <= slot) & (key_slot >= first), 0.0, NEG
        )
    key_sum[...] = jnp.zeros_like(key_sum)
    value_sum[...] = jnp.zeros_like(value_sum)
    bias[...] = jnp.zeros_like(bias)

    def pick(own, far, g):
        found = []
        for k in range(pack):
            at = pl.ds(pl.multiple_of((g + k) * HD, HD), HD)
            found += [own[:, at], far[:, at]]
        return jnp.concatenate(found, axis=0)

    def heads(j, _):
        g = j * pack
        query = pick(query_own, query_far, g)
        grad = pick(grad_own, grad_far, g)
        score_ref[...] = nn(query, key_t[...])
        press_ref[...] = nn(grad, value_t[...])
        span = CORES * length
        for r in range(0, pack * span, ROW_TILE):
            rows = slice(r, r + ROW_TILE)
            at = slice(r % span, r % span + ROW_TILE)
            score = score_ref[rows, :] * (scaling * LOG2E) + mask[at, :]
            raw = jnp.exp2(score - jnp.max(score, axis=1, keepdims=True))
            prob = raw * (1.0 / jnp.sum(raw, axis=1, keepdims=True))
            press = press_ref[rows, :]
            centred = jnp.sum(prob * press, axis=1, keepdims=True)
            weight_ref[rows, :] = prob.astype(jnp.bfloat16)
            slope_ref[rows, :] = (prob * (press - centred)).astype(jnp.bfloat16)
        weight = weight_ref[...]
        slope = slope_ref[...]
        out = nn(weight, gathered(length)).astype(jnp.bfloat16)
        into = (nn(slope, gathered(0)) * scaling).astype(jnp.bfloat16)
        for k in range(pack):
            at = pl.ds(pl.multiple_of((g + k) * HD, HD), HD)
            near = slice(k * span, k * span + length)
            away = slice(k * span + length, (k + 1) * span)
            attended[:, at] = out[near]
            grad_query[:, at] = into[near]
            far_out[0, :, at] = out[away]
            far_out[1, :, at] = into[away]
            total = jnp.sum(into[k * span : (k + 1) * span].astype(jnp.float32), axis=0)
            bias[pl.ds(g + k, 1), :] = total[None]
        key_sum[...] += nn(query.T, slope)
        value_sum[...] += nn(grad.T, weight)
        return 0

    lax.fori_loop(0, GROUP // pack, heads, 0)
    from_values = value_sum[...]
    bias[GROUP : GROUP + 1, :] = lying(jnp.sum(from_values, axis=1, keepdims=True))
    from_keys = (key_sum[...] * scaling).astype(jnp.bfloat16)
    from_values = from_values.astype(jnp.bfloat16)
    for r in range(count):
        cols = slice(r * length, (r + 1) * length)
        if split:
            parts[r // CORES][r % CORES, :HD, :] = from_keys[:, cols]
            parts[r // CORES][r % CORES, HD:, :] = from_values[:, cols]
        else:
            parts[0][index ^ r, :HD, :] = from_keys[:, cols]
            parts[0][index ^ r, HD:, :] = from_values[:, cols]


def attention(index, chunk, chunks, plan, rows_in, pairs, carried, split):
    count = plan.shape[0]
    chips = count // CORES
    length, width = rows_in[-1].shape
    wide = GROUP * HD
    whole = lambda *shape: pl.BlockSpec(shape, lambda i, c: (0,) * len(shape))
    mine = pl.BlockSpec((length, wide), lambda i, c: (0, chunks * (c[0] % CORES) + chunk))
    out_shape = [
        jax.ShapeDtypeStruct((length, width), jnp.bfloat16),
        jax.ShapeDtypeStruct((length, width), jnp.bfloat16),
        jax.ShapeDtypeStruct((chunks * BIAS_ROWS, HD), jnp.float32),
        jax.ShapeDtypeStruct((2, length, chunks * wide), jnp.bfloat16),
    ]
    part = (CORES, 2 * HD, length) if split else (count, 2 * HD, length)
    parts = chips if split else 1
    out_shape += [jax.ShapeDtypeStruct(part, jnp.bfloat16)] * parts
    rows = CORES * length
    cols = count * length
    far = pl.BlockSpec((2, length, wide), lambda i, c: (0, 0, chunk))
    near = pl.BlockSpec((length, wide), lambda i, c: (0, chunk))
    in_specs = [whole(*plan.shape), near, near, mine, mine]
    in_specs += [whole(*pairs[0].shape)] * len(pairs)
    operands = [plan, *rows_in, *pairs]
    aliases = {}
    if carried is not None:
        in_specs += [pl.BlockSpec(memory_space=pl.ANY)] * 4
        aliases = {6 + len(pairs) + k: k for k in range(4)}
        operands += list(carried)
    pack = GROUP
    while pack > 1 and pack * rows * cols > 2 * 1024 * 1024:
        pack //= 2
    grid_spec = pltpu.PrefetchScalarGridSpec(
        num_scalar_prefetch=1,
        grid=(1,),
        in_specs=in_specs,
        out_specs=[
            mine,
            mine,
            pl.BlockSpec((BIAS_ROWS, HD), lambda i, c: (chunk, 0)),
            far,
        ]
        + [whole(*part)] * parts,
        scratch_shapes=[
            pltpu.VMEM((HD, cols), jnp.bfloat16),
            pltpu.VMEM((HD, cols), jnp.bfloat16),
            pltpu.VMEM((rows, cols), jnp.float32),
            pltpu.VMEM((HD, cols), jnp.float32),
            pltpu.VMEM((HD, cols), jnp.float32),
        ]
        + [pltpu.VMEM((pack * rows, cols), jnp.float32)] * 2
        + [pltpu.VMEM((pack * rows, cols), jnp.bfloat16)] * 2
        + [],
    )
    work = rows * GROUP * cols
    return pl.pallas_call(
        functools.partial(
            attention_kernel,
            carried=carried is not None,
            split=split,
            joined=len(pairs) == chips,
        ),
        grid_spec=grid_spec,
        out_shape=out_shape,
        input_output_aliases=aliases,
        compiler_params=pltpu.CompilerParams(
            vmem_limit_bytes=min(60, VMEM_MIB * cols // 1024) * 1024 * 1024
        ),
        cost_estimate=pl.CostEstimate(
            flops=12 * work * HD, transcendentals=work, bytes_accessed=8 * length * wide * 2
        ),
        name="attention",
    )(index, *operands)


def payload_kernel(index_ref, first_ref, keys, values, *outs):
    length = keys.shape[0]
    chunks = len(outs) // CORES
    index = index_ref[0]
    linked = (first_ref[0, 0] < index).astype(jnp.float32)
    flags = jnp.full((EXTRA, HD), linked, jnp.float32).astype(jnp.bfloat16)
    even = index % CORES == 0
    for hh in range(chunks):
        near, away = outs[CORES * hh : CORES * (hh + 1)]
        heads = [slice((c * chunks + hh) * HD, (c * chunks + hh + 1) * HD) for c in range(CORES)]
        for at, source in ((0, keys), (length, values)):
            first, second = source[:, heads[0]], source[:, heads[1]]
            near[at : at + length, :] = jnp.where(even, first, second)
            away[at : at + length, :] = jnp.where(even, second, first)
        near[2 * length :, :] = flags
        away[2 * length :, :] = flags


def payload(index, group_first, keys, values, chunks):
    length = keys.shape[0]
    smem = pl.BlockSpec(memory_space=pltpu.SMEM)
    vmem = pl.BlockSpec(memory_space=pltpu.VMEM)
    shape = jax.ShapeDtypeStruct((2 * length + EXTRA, HD), jnp.bfloat16)
    return pl.pallas_call(
        payload_kernel,
        in_specs=[smem, smem, vmem, vmem],
        out_shape=[shape] * (CORES * chunks),
        name="payload",
    )(index, group_first, keys, values)


def place_kernel(index_ref, far, piece, *refs):
    attended, grad_query, grad_key, grad_value = refs[-4:]
    attended[...] = far[0]
    grad_query[...] = far[1]
    grad_key[...] = piece[:HD].astype(jnp.float32).T.astype(jnp.bfloat16)
    grad_value[...] = piece[HD:].astype(jnp.float32).T.astype(jnp.bfloat16)


def place(index, chunk, chunks, far, piece, filled):
    _, length, half = far.shape
    theirs = pl.BlockSpec((length, half), lambda i, c: (0, 1 - c[0] % CORES))
    head = pl.BlockSpec((length, HD), lambda i, c: (0, (1 - c[0] % CORES) * chunks + chunk))
    grid_spec = pltpu.PrefetchScalarGridSpec(
        num_scalar_prefetch=1,
        grid=(1,),
        in_specs=[
            pl.BlockSpec(far.shape, lambda i, c: (0, 0, 0)),
            pl.BlockSpec(piece.shape, lambda i, c: (0, 0)),
        ]
        + [pl.BlockSpec(memory_space=pl.ANY)] * 4,
        out_specs=[theirs, theirs, head, head],
    )
    return pl.pallas_call(
        place_kernel,
        grid_spec=grid_spec,
        out_shape=[jax.ShapeDtypeStruct(x.shape, x.dtype) for x in filled],
        input_output_aliases={3 + k: k for k in range(4)},
        compiler_params=pltpu.CompilerParams(vmem_limit_bytes=8 * 1024 * 1024),
        name="place",
    )(index, far, piece, *filled)


def added(pieces):
    total = pieces[0].astype(jnp.float32)
    for piece in pieces[1:]:
        total = total + piece.astype(jnp.float32)
    return total


def settle_kernel(index_ref, *refs, count):
    grad_key, grad_value, away = refs[-3:]
    total = added([piece[0] for piece in refs[:count]])
    grad_key[...] = total[:HD].T.astype(jnp.bfloat16)
    grad_value[...] = total[HD:].T.astype(jnp.bfloat16)
    away[...] = added([piece[1] for piece in refs[:count]]).astype(jnp.bfloat16)


def into_grads(kernel, index, grid, specs, operands, heads, shape, extra, carried):
    specs = list(specs)
    aliases = {}
    if carried is not None:
        specs += [pl.BlockSpec(memory_space=pl.ANY)] * 2
        aliases = {1 + len(operands): 0, 2 + len(operands): 1}
        operands = [*operands, *carried]
    block = pl.BlockSpec((shape[0], HD), heads)
    out_specs = [block, block]
    out_shape = [jax.ShapeDtypeStruct(shape, jnp.bfloat16)] * 2
    if extra is not None:
        out_specs.append(pl.BlockSpec(extra, lambda i, c: (0,) * len(extra)))
        out_shape.append(jax.ShapeDtypeStruct(extra, jnp.bfloat16))
    grid_spec = pltpu.PrefetchScalarGridSpec(
        num_scalar_prefetch=1, grid=(grid,), in_specs=specs, out_specs=out_specs
    )
    return pl.pallas_call(
        kernel,
        grid_spec=grid_spec,
        out_shape=out_shape,
        input_output_aliases=aliases,
        compiler_params=pltpu.CompilerParams(vmem_limit_bytes=8 * 1024 * 1024),
    )(index, *operands)


def settle(index, chunk, chunks, pieces, shape, carried):
    spec = pl.BlockSpec(pieces[0].shape, lambda i, c: (0, 0, 0))
    heads = lambda i, c: (0, (c[0] % CORES) * chunks + chunk)
    kernel = functools.partial(settle_kernel, count=len(pieces))
    extra = pieces[0].shape[1:]
    return into_grads(kernel, index, 1, [spec] * len(pieces), pieces, heads, shape, extra, carried)


def last_kernel(index_ref, sums, piece, *refs, chunks, factor):
    grad_key, grad_value, bias_grad = refs[-3:]
    grad_key[...] = piece[:HD].astype(jnp.float32).T.astype(jnp.bfloat16)
    grad_value[...] = piece[HD:].astype(jnp.float32).T.astype(jnp.bfloat16)
    core = index_ref[0] % CORES
    for c in range(CORES):
        ours = core == c
        for hh in range(chunks):
            head = c * chunks + hh
            rows = slice(hh * BIAS_ROWS, hh * BIAS_ROWS + GROUP)
            bias_grad[head * GROUP : (head + 1) * GROUP, :] = (
                jnp.where(ours, sums[0, rows, :], sums[1, rows, :]) * factor
            )
            row = slice(hh * BIAS_ROWS + GROUP, hh * BIAS_ROWS + GROUP + 1)
            at = CORES * chunks * GROUP + head
            bias_grad[at : at + 1, :] = (
                jnp.where(ours, sums[0, row, :], sums[1, row, :]) * factor
            )


def last(index, sums, chunk, chunks, piece, grads, factor):
    length = grads[0].shape[0]
    head = pl.BlockSpec((length, HD), lambda i, c: (0, (1 - c[0] % CORES) * chunks + chunk))
    bias_shape = (CORES * chunks * (GROUP + 1), HD)
    grid_spec = pltpu.PrefetchScalarGridSpec(
        num_scalar_prefetch=1,
        grid=(1,),
        in_specs=[
            pl.BlockSpec(sums.shape, lambda i, c: (0, 0, 0)),
            pl.BlockSpec(piece.shape, lambda i, c: (0, 0)),
        ]
        + [pl.BlockSpec(memory_space=pl.ANY)] * 2,
        out_specs=[head, head, pl.BlockSpec(bias_shape, lambda i, c: (0, 0))],
    )
    return pl.pallas_call(
        functools.partial(last_kernel, chunks=chunks, factor=factor),
        grid_spec=grid_spec,
        out_shape=[jax.ShapeDtypeStruct(x.shape, x.dtype) for x in grads]
        + [jax.ShapeDtypeStruct(bias_shape, jnp.float32)],
        input_output_aliases={3: 0, 4: 1},
        compiler_params=pltpu.CompilerParams(vmem_limit_bytes=8 * 1024 * 1024),
        name="last",
    )(index, sums, piece, *grads)


def summed(part, axis, steps):
    size = lax.axis_size(axis)
    if len(steps) > 2:
        for step in steps:
            part = part + lax.ppermute(part, axis, [(i, i ^ step) for i in range(size)])
        return part
    total = part
    for pick in range(1, 2 ** len(steps)):
        mixed = sum(step for k, step in enumerate(steps) if pick >> k & 1)
        moved = lax.ppermute(part, axis, [(i, i ^ mixed) for i in range(size)])
        total = total + moved
    return total


def powers(start, stop):
    found = []
    while start < stop:
        found.append(start)
        start *= 2
    return found


def body(query_rows, key_rows, value_rows, out_grad, destination, group_first):
    length = query_rows.shape[0]
    devices = lax.axis_size("ctx")
    replicas = lax.axis_size("dp")
    index = lax.axis_index("ctx").astype(jnp.int32)
    kv_heads = key_rows.shape[1] // HD
    chunks = kv_heads // CORES
    plan = destination.reshape(devices, length)
    across = [(i, i ^ 1) for i in range(devices)]
    index_arg = index.reshape(1)

    chips = devices // CORES
    order = range(chips - 1, 0, -1)

    def over(k):
        return [(i, i ^ (CORES * k)) for i in range(devices)]

    def xor(r):
        return [(i, i ^ r) for i in range(devices)]

    query_far = lax.ppermute(query_rows, "ctx", across)
    grad_far = lax.ppermute(out_grad, "ctx", across)
    half = query_rows.shape[1] // CORES
    begin = (index % CORES) * half
    near = [lax.dynamic_slice_in_dim(rows, begin, half, axis=1) for rows in (query_rows, out_grad)]
    rows_in = (*near, query_far, grad_far)
    blocks = payload(index_arg, group_first, key_rows, value_rows, chunks)
    gathered = []
    for hh in range(chunks):
        mine = blocks[CORES * hh : CORES * (hh + 1)]
        if JOIN[hh % len(JOIN)]:
            away = lax.ppermute(mine[1], "ctx", across)
            both = jnp.stack([mine[0], away])
            pairs = [both] * chips
            for k in order:
                pairs[k] = lax.ppermute(both, "ctx", over(k))
        else:
            pairs = [mine[0]] * devices
            for r in range(devices - 1, 0, -1):
                pairs[r] = lax.ppermute(mine[r % CORES], "ctx", xor(r))
        gathered.append(pairs)
    carried = None
    returned = []
    for hh in range(chunks):
        outs = attention(
            index_arg,
            hh,
            chunks,
            plan,
            rows_in,
            gathered[hh],
            carried,
            True,
        )
        carried, parts = outs[:4], outs[4:]
        pieces = list(parts)
        for k in order:
            pieces[k] = lax.ppermute(parts[k], "ctx", over(k))
        returned.append(pieces)
    attended, grad_query, bias, far_out = carried
    far_out = lax.ppermute(far_out, "ctx", across)
    both = jnp.stack([bias, lax.ppermute(bias, "ctx", across)])
    both = summed(both, "dp", powers(1, replicas))
    both = summed(both, "ctx", powers(CORES, devices))
    factor = 1.0 / math.sqrt(length * devices * replicas)
    grads = None
    crossed = []
    for hh in range(chunks):
        *grads, away = settle(index_arg, hh, chunks, returned[hh], key_rows.shape, grads)
        crossed.append(lax.ppermute(away, "ctx", across))
    for hh in range(chunks - 1):
        attended, grad_query, *grads = place(
            index_arg, hh, chunks, far_out, crossed[hh], (attended, grad_query, *grads)
        )
    away = crossed[-1]
    *grads, bias_grad = last(index_arg, both, chunks - 1, chunks, away, grads, factor)
    return (attended, grad_query, *grads, bias_grad.reshape(-1))


def solution(mesh):
    rows = P(("dp", "ctx"), None)
    return jax.shard_map(
        body,
        mesh=mesh,
        in_specs=(rows, rows, rows, rows, P("dp", None), P("dp", "ctx")),
        out_specs=(rows, rows, rows, rows, P()),
        check_vma=False,
    )
```
